128 devices in a mesh: gx: 16 (over y, x), gy: 8 (over z, core).
Axes of the slice: x: 4, y: 4, z: 4, core: 2. Of those that a mesh axis runs over, the one named last changes fastest.
Arguments:
- adjoint: float32 [40, 16, 128, 1024], P(None, None, 'gx', 'gy'), may hold values from -6 to 6
- concentration: float32 [40, 16, 128, 1024], P(None, None, 'gx', 'gy'), may hold values from 0.1 to 2
- courant_x: float32 [16, 128, 1024], P(None, 'gx', 'gy'), may hold values from -0.3 to 0.3
- courant_y: float32 [16, 128, 1024], P(None, 'gx', 'gy'), may hold values from -0.3 to 0.3
- diffusion: float32 [16], replicated, may hold values from 0.02 to 0.1
- coag_kernel: float32 [40, 40], replicated, may hold values from 0.005 to 0.03
- pixel_column: int32 [262144], P(('gx', 'gy')), may hold values from 0 to 1023
- pixel_owner: int32 [262144, 1], P(('gx', 'gy')), may hold values from 0 to 127; in each aligned block of 2048 rows (0 to 2047, 2048 to 4095, ...) at most 64 rows name the same one
- pixel_slot: int32 [262144], P(('gx', 'gy')), may hold values from 0 to 127
- pixel_level: int32 [262144], P(('gx', 'gy')), may hold values from 0 to 15
- pixel_weight: float32 [262144], P(('gx', 'gy')), may hold values from 0.2 to 1
Outputs:
- adjoint_next: float32 [40, 16, 128, 1024], P(None, None, 'gx', 'gy')
- emission_gradient: float32 [40, 16384], P(None, ('gx', 'gy'))
The draws below stay inside these ranges and needn't reach their ends.
Inputs may be any that keep to these rules, and one draw needn't show every extreme that they name: `pixel_column`: column a * 128 + b is the column a along the east-west and b along the north-south dimension of the tile of the device that holds the row. `pixel_owner`: among the rows of one device, no owner appears more than 64 times.
All inputs are finite; a program needn't handle non-finite values.
Results may differ from the reference program's by a relative error of at most 0.000076.
Values sent between devices are 32-bit elements; how exact they have to be, the bound alone decides.
A program may use at most 128 MiB of HBM per device.

```python
import math
import jax
import jax.numpy as jnp
import numpy as np
from jax import lax

SEC = 40
LEV = 16
CX = 8
CY = 128
PIX_DEV = 2048
DET_DEV = 128
NX = 128
NY = 1024
PIXELS = 262144
CAP = 64
N_GY = 8
DEVICES = 128


def place_ends(entries, stream_key, least, largest):
    longest = entries.shape.index(max(entries.shape))
    spots = []
    for shift in (0, 1):
        where = [jax.random.randint(jax.random.fold_in(stream_key, axis), (), 0, length) for axis, length in enumerate(entries.shape)]
        where[longest] = (where[longest] + shift) % entries.shape[longest]
        spots.append(tuple(where))
    return entries.at[spots[0]].set(least).at[spots[1]].set(largest)


def steps_of(stream_key, dims, shards, smallest, high):
    def one(axis_at, shards_of):
        steps = jax.random.uniform(jax.random.fold_in(jax.random.fold_in(stream_key, 6), axis_at), (shards_of,), jnp.float32, smallest / len(shards), high / len(shards))
        return jnp.repeat(jnp.exp(steps), dims[axis_at] // shards_of).reshape((-1,) + (1,) * (len(dims) - axis_at - 1))

    factor_of = one(*shards[0])
    for cut in shards[1:]:
        factor_of = factor_of * one(*cut)
    return factor_of


def routed_block(key, own, number, rows, number_of, top, bound, slope):
    sequence = jax.random.permutation(key, number_of)
    heavy_load, common = load_shares(number_of, rows * top, bound, slope, True), load_shares(number_of, rows * top, bound, slope, False)
    places = jnp.arange(number_of)

    def named(sizes, offset_by):
        used = int((sizes > 0).sum())
        fixed = max(1, used // 4)
        shifted = fixed + (places - fixed + offset_by * (used - fixed)) % max(1, number_of - fixed)
        return jnp.zeros((number_of,), jnp.int32).at[sequence[jnp.where(places < fixed, places, shifted)]].set(jnp.asarray(sizes, jnp.int32))

    sizes = jnp.where(number % 4 == 0, named(heavy_load, number // 4), named(common, number - number // 4 - 1))
    mixed = jax.random.permutation(jax.random.fold_in(own, 3), number_of)
    giver, receiver = mixed[0:number_of // 2 * 2:2], mixed[1:number_of // 2 * 2:2]
    slack = jnp.minimum(sizes[giver] - 1, bound - sizes[receiver]) // 2
    slack = jnp.where((giver == sequence[0]) | (receiver == sequence[0]) | (sizes[receiver] == 0), 0, jnp.maximum(slack, 0))
    shifted = jax.random.randint(jax.random.fold_in(own, 4), (number_of // 2,), 0, 1 << 20) % (slack + 1)
    sizes = sizes.at[giver].add(-shifted).at[receiver].add(shifted)
    members = jnp.searchsorted(jnp.cumsum(sizes), jnp.arange(rows * top), side="right").astype(jnp.int32)
    listing = members.reshape(top, rows).T
    listing = listing[jax.random.permutation(jax.random.fold_in(own, 1), rows)]
    offset_by = jax.random.randint(jax.random.fold_in(own, 2), (rows, 1), 0, top)
    return jnp.take_along_axis(listing, (jnp.arange(top)[None, :] + offset_by) % top, axis=1)


def load_shares(number_of, total, limit, skew, full):
    loads = [(1 << 20) // math.isqrt(grade ** skew) + 1 for grade in range(1, number_of + 1)]
    largest = limit if full else min(limit, max(-(-total // number_of), total * loads[0] // sum(loads)))
    least = 1 if total - largest >= number_of - 1 else 0
    counts, spare = [largest] + [least] * (number_of - 1), total - largest - least * (number_of - 1)
    while spare > 0:
        movable = [i for i in range(1, number_of) if counts[i] < largest] or [i for i in range(1, number_of) if counts[i] < limit]
        mass, budget = sum([loads[i] for i in movable]), spare
        for i in movable:
            addition = min(limit - counts[i], max(1, budget * loads[i] // mass), spare)
            counts[i] = counts[i] + addition
            spare = spare - addition
    return np.array(counts)


def scatter_about(rng, shape, spread, most, shards=(), held_as=jnp.bfloat16):
    level = steps_of(rng, shape, shards, -0.22, 0.18) if shards else 1.0
    values = jax.random.normal(rng, shape, jnp.float32) * spread * level
    return jnp.minimum(jnp.maximum(values, -most), most).astype(held_as)


def setup_inputs(seed: int = 0) -> dict:
    keys = jax.random.split(jax.random.key(seed), 12)
    adjoint = scatter_about(keys[0], (SEC, LEV, NX, NY), 1.0, 6.0, ((2, 16), (3, 8)), jnp.float32)
    concentration = jnp.clip(jnp.exp(math.log(2.0) - 2.9957323 * jax.random.uniform(keys[1], (SEC, LEV, NX, NY), jnp.float32) ** steps_of(keys[1], (SEC, LEV, NX, NY), ((2, 16), (3, 8)), -0.2, 0.2)), 0.1, 2.0)
    courant_x = jnp.clip(jax.random.uniform(keys[2], (LEV, NX, NY), jnp.float32, -0.3, 0.3) * steps_of(keys[2], (LEV, NX, NY), ((1, 16), (2, 8)), -0.4, 0.0), -0.3, 0.3)
    courant_y = jnp.clip(jax.random.uniform(keys[3], (LEV, NX, NY), jnp.float32, -0.3, 0.3) * steps_of(keys[3], (LEV, NX, NY), ((1, 16), (2, 8)), -0.4, 0.0), -0.3, 0.3)
    diffusion = jnp.clip(jax.random.uniform(keys[4], (LEV,), jnp.float32, 0.02, 0.1), 0.02, 0.1)
    coag_kernel = jnp.clip(jax.random.uniform(keys[5], (SEC, SEC), jnp.float32, 0.005, 0.03), 0.005, 0.03)
    pixel_column = place_ends(jax.random.randint(keys[6], (PIXELS,), 0, CX * CY), jax.random.fold_in(keys[6], 1), 0, (CX * CY) - 1).astype(jnp.int32)
    pixel_owner_keys = jax.random.split(jax.random.fold_in(keys[7], 1), PIXELS // PIX_DEV)
    pixel_owner_turns = jax.random.permutation(jax.random.fold_in(keys[7], 3), PIXELS // PIX_DEV)
    pixel_owner = jax.vmap(lambda own, number: routed_block(jax.random.fold_in(keys[7], 2), own, number, PIX_DEV, DEVICES, 1, CAP, 2))(pixel_owner_keys, pixel_owner_turns).reshape((PIXELS, 1))
    pixel_slot = place_ends(jax.random.randint(keys[8], (PIXELS,), 0, DET_DEV), jax.random.fold_in(keys[8], 1), 0, DET_DEV - 1).astype(jnp.int32)
    pixel_level = place_ends(jax.random.randint(keys[9], (PIXELS,), 0, LEV), jax.random.fold_in(keys[9], 1), 0, LEV - 1).astype(jnp.int32)
    pixel_weight = jnp.clip(0.2 + 0.8 * jax.random.uniform(keys[10], (PIXELS,), jnp.float32) ** steps_of(keys[10], (PIXELS,), ((0, 128),), -0.2, 0.2), 0.2, 1.0)
    return {"adjoint": adjoint, "concentration": concentration, "courant_x": courant_x, "courant_y": courant_y, "diffusion": diffusion, "coag_kernel": coag_kernel, "pixel_column": pixel_column, "pixel_owner": pixel_owner, "pixel_slot": pixel_slot, "pixel_level": pixel_level, "pixel_weight": pixel_weight}


def transport(lam_pad, cx_pad, cy_pad, kappa_lev):
    centre = lam_pad[..., 1:-1, 1:-1]
    east = lam_pad[..., 2:, 1:-1]
    west = lam_pad[..., :-2, 1:-1]
    north = lam_pad[..., 1:-1, 2:]
    south = lam_pad[..., 1:-1, :-2]
    keep = 1.0 - jnp.abs(cx_pad[..., 1:-1, 1:-1]) - jnp.abs(cy_pad[..., 1:-1, 1:-1]) - 4.0 * kappa_lev
    moved = keep * centre
    moved = moved + jnp.maximum(cx_pad[..., 2:, 1:-1], 0.0) * east
    moved = moved + jnp.maximum(-cx_pad[..., :-2, 1:-1], 0.0) * west
    moved = moved + jnp.maximum(cy_pad[..., 1:-1, 2:], 0.0) * north
    moved = moved + jnp.maximum(-cy_pad[..., 1:-1, :-2], 0.0) * south
    return moved + kappa_lev * (east + west + north + south)


def coagulate(moved, concentration, coag_kernel):
    sections = moved.shape[0]
    flat_lam = moved.reshape(sections, -1)
    flat_conc = concentration.reshape(sections, -1)
    rate = jnp.dot(coag_kernel, flat_conc, precision=lax.Precision.HIGHEST, preferred_element_type=jnp.float32)
    upper = jnp.concatenate([flat_lam[1:], jnp.zeros_like(flat_lam[:1])], axis=0) - flat_lam
    back = jnp.dot(coag_kernel.T, upper * flat_conc, precision=lax.Precision.HIGHEST, preferred_element_type=jnp.float32)
    return (flat_lam + upper * rate + back).reshape(moved.shape)


def plume_profile(level_ids, levels):
    heights = jnp.arange(levels, dtype=jnp.float32)[:, None] - level_ids[None, :].astype(jnp.float32)
    weights = jnp.exp(-heights * heights / 8.0)
    return weights / jnp.sum(weights, axis=0, keepdims=True)


def reference(adjoint, concentration, courant_x, courant_y, diffusion, coag_kernel, pixel_column, pixel_owner, pixel_slot, pixel_level, pixel_weight):
    kappa_lev = diffusion[:, None, None]
    cx_pad = jnp.pad(courant_x, ((0, 0), (1, 1), (1, 1)))
    cy_pad = jnp.pad(courant_y, ((0, 0), (1, 1), (1, 1)))

    def one_section(field):
        return transport(jnp.pad(field, ((0, 0), (1, 1), (1, 1))), cx_pad, cy_pad, kappa_lev)

    moved = lax.map(one_section, adjoint)
    adjoint_next = coagulate(moved, concentration, coag_kernel)
    count = pixel_column.shape[0]
    block_ids = jnp.arange(count, dtype=jnp.int32) // PIX_DEV
    east_ids = (block_ids // N_GY) * CX + pixel_column // CY
    north_ids = (block_ids % N_GY) * CY + pixel_column % CY
    profile = plume_profile(pixel_level, LEV)
    contrib = jnp.zeros((SEC, count), jnp.float32)
    for level in range(LEV):
        contrib = contrib + profile[level][None, :] * adjoint_next[:, level, east_ids, north_ids]
    contrib = contrib * pixel_weight[None, :]
    target = pixel_owner[:, 0] * DET_DEV + pixel_slot
    gradient = jax.ops.segment_sum(contrib.T, target, num_segments=DET_DEV * DEVICES).T
    return adjoint_next, gradient
```

```python
import jax
import jax.numpy as jnp
from jax import lax
from jax.experimental import pallas as pl
from jax.experimental.pallas import tpu as pltpu
from jax.sharding import PartitionSpec as P

MESH = pl.DeviceIdType.MESH
F32 = jnp.float32
BF16 = jnp.bfloat16
SEC, LEV, CX, CY = 40, 16, 8, 128
PIX = 2048
LCH = 4
TILE = 256
BANDS = ((0, 16), (16, 16), (32, 8))


def split(v):
    hi = v.astype(BF16).astype(F32)
    return hi, v - hi


def place():
    gx = lax.axis_index("gx")
    gy = lax.axis_index("gy")
    return lax.rem(gx, 4), gx // 4, gy // 2, lax.rem(gy, 2)


def halo_kernel(kap_ref, adj_ref, cx_ref, cy_ref, out_x, out_y, px, py, rx, ry, ssem, rsem):
    gx = lax.axis_index("gx")
    gy = lax.axis_index("gy")
    peers = (
        (lax.rem(gx + 15, 16), gy),
        (lax.rem(gx + 1, 16), gy),
        (gx, lax.rem(gy + 7, 8)),
        (gx, lax.rem(gy + 1, 8)),
    )
    barrier = pltpu.get_barrier_semaphore()
    for peer in peers:
        pl.semaphore_signal(barrier, 1, device_id=peer, device_id_type=MESH)
    kap = kap_ref[...]
    first = jnp.maximum(cx_ref[:, 0, :], 0.0) + kap
    last = jnp.maximum(-cx_ref[:, CX - 1, :], 0.0) + kap

    def fill(k, c):
        px[0, k] = adj_ref[k, :, 0, :] * first
        px[1, k] = adj_ref[k, :, CX - 1, :] * last
        return c

    lax.fori_loop(0, SEC, fill, 0)
    pl.semaphore_wait(barrier, 4)
    copies = [
        pltpu.make_async_remote_copy(
            px.at[i], rx.at[i], ssem.at[i], rsem.at[i], device_id=peers[i], device_id_type=MESH
        )
        for i in range(2)
    ]
    for c in copies:
        c.start()
    lane = lax.broadcasted_iota(jnp.int32, (SEC, CY), 1)

    def edge(l, carry):
        low, high = carry
        for x in range(CX):
            a = adj_ref[:, l, x, :]
            cyr = cy_ref[l, pl.ds(x, 1), :]
            kp = kap_ref[pl.ds(l, 1), :]
            q = l * CX + x
            s = pltpu.roll(a * (jnp.maximum(cyr, 0.0) + kp), q, 1)
            n = pltpu.roll(a * (jnp.maximum(-cyr, 0.0) + kp), q + 1, 1)
            low = jnp.where(lane == q, s, low)
            high = jnp.where(lane == q, n, high)
        return low, high

    zero = jnp.zeros((SEC, CY), F32)
    low, high = lax.fori_loop(0, LEV, edge, (zero, zero))
    py[0] = low
    py[1] = high
    more = [
        pltpu.make_async_remote_copy(
            py.at[i],
            ry.at[i],
            ssem.at[2 + i],
            rsem.at[2 + i],
            device_id=peers[2 + i],
            device_id_type=MESH,
        )
        for i in range(2)
    ]
    for c in more:
        c.start()
    for c in more:
        c.wait()
    out_y[0] = jnp.where(gy == 7, 0.0, ry[0])
    out_y[1] = jnp.where(gy == 0, 0.0, ry[1])
    for c in copies:
        c.wait()
    out_x[0] = jnp.where(gx == 15, 0.0, rx[0])
    out_x[1] = jnp.where(gx == 0, 0.0, rx[1])


def halos(kap, adjoint, courant_x, courant_y):
    vmem = pl.BlockSpec(memory_space=pltpu.VMEM)
    return pl.pallas_call(
        halo_kernel,
        out_shape=(
            jax.ShapeDtypeStruct((2, SEC, LEV, CY), F32),
            jax.ShapeDtypeStruct((2, SEC, CY), F32),
        ),
        in_specs=[vmem] * 4,
        out_specs=(vmem, vmem),
        scratch_shapes=[
            pltpu.VMEM((2, SEC, LEV, CY), F32),
            pltpu.VMEM((2, SEC, CY), F32),
            pltpu.VMEM((2, SEC, LEV, CY), F32),
            pltpu.VMEM((2, SEC, CY), F32),
            pltpu.SemaphoreType.DMA((4,)),
            pltpu.SemaphoreType.DMA((4,)),
        ],
        compiler_params=pltpu.CompilerParams(
            collective_id=0, has_side_effects=True, vmem_limit_bytes=48 << 20
        ),
    )(kap, adjoint, courant_x, courant_y)


def local_kernel(
    kap_ref, adj_ref, conc_ref, cx_ref, cy_ref, hx_ref, hy_ref, ker_ref, kert_ref,
    pix_ref, wgt_ref, out_ref, dense_ref, held, contrib,
):
    l = pl.program_id(0)
    lane = lax.broadcasted_iota(jnp.int32, (SEC, CY), 1)
    row = lax.broadcasted_iota(jnp.int32, (SEC, CY), 0)
    kap = kap_ref[pl.ds(l, 1), :]
    hn = pltpu.roll(hy_ref[0], lax.rem(CY - l * CX, CY), 1)
    hs = pltpu.roll(hy_ref[1], lax.rem(CY - l * CX, CY), 1)
    adj = [adj_ref[:, 0, x, :] for x in range(CX)]
    cxr = [cx_ref[0, pl.ds(x, 1), :] for x in range(CX)]
    moved, ups, concs = [], [], []
    for x in range(CX):
        cyr = cy_ref[0, pl.ds(x, 1), :]
        a = adj[x]
        m = (1.0 - jnp.abs(cxr[x]) - jnp.abs(cyr) - 4.0 * kap) * a
        if x < CX - 1:
            m = m + (jnp.maximum(cxr[x + 1], 0.0) + kap) * adj[x + 1]
        else:
            m = m + hx_ref[0, :, l, :]
        if x > 0:
            m = m + (jnp.maximum(-cxr[x - 1], 0.0) + kap) * adj[x - 1]
        else:
            m = m + hx_ref[1, :, l, :]
        north = (jnp.maximum(cyr, 0.0) + kap) * a
        south = (jnp.maximum(-cyr, 0.0) + kap) * a
        nh = pltpu.roll(hn, (CY - x) % CY, 1)
        sh = pltpu.roll(hs, (CY - 1 - x) % CY, 1)
        m = m + pltpu.roll(jnp.where(lane == 0, nh, north), CY - 1, 1)
        m = m + pltpu.roll(jnp.where(lane == CY - 1, sh, south), 1, 1)
        nxt = jnp.where(row == SEC - 1, 0.0, pltpu.roll(m, SEC - 1, 0))
        moved.append(m)
        ups.append(nxt - m)
        concs.append(conc_ref[:, 0, x, :])
    m = jnp.concatenate(moved, axis=1)
    up = jnp.concatenate(ups, axis=1)
    cc = jnp.concatenate(concs, axis=1)

    def product(k, v):
        kh, kl = split(k)
        vh, vl = split(v)
        k3 = jnp.concatenate([kh, kh, kl], axis=1).astype(BF16)
        v3 = jnp.concatenate([vh, vl, vh], axis=0).astype(BF16)
        return jnp.dot(k3, v3, preferred_element_type=F32)

    rate = product(ker_ref[...], cc)
    back = product(kert_ref[...], up * cc)
    res = m + up * rate + back
    for x in range(CX):
        out_ref[:, 0, x, :] = res[:, x * CY:(x + 1) * CY]
    rh, rl = split(res)
    held[l] = jnp.concatenate([rh, rl], axis=0).astype(BF16)

    @pl.when(l == LEV - 1)
    def _():
        cells = lax.broadcasted_iota(jnp.int32, (CX * CY, TILE), 0)

        def gather(t, c):
            at = pl.ds(pl.multiple_of(t * TILE, TILE), TILE)
            onehot = jnp.where(cells == pix_ref[pl.ds(0, 1), at], 1.0, 0.0).astype(BF16)
            plev = pix_ref[pl.ds(1, 1), at].astype(F32)
            height = lax.broadcasted_iota(jnp.int32, (LEV, TILE), 0).astype(F32) - plev
            prof = jnp.exp(-height * height / 8.0)
            prof = prof / jnp.sum(prof, axis=0, keepdims=True) * wgt_ref[:, at]
            total = jnp.zeros((SEC, TILE), F32)
            for j in range(LEV // LCH):
                block = held[pl.ds(j * LCH, LCH)].reshape(LCH * 2 * SEC, CX * CY)
                got = jnp.dot(block, onehot, preferred_element_type=F32)
                for i in range(LCH):
                    base = i * 2 * SEC
                    both = got[base:base + SEC] + got[base + SEC:base + 2 * SEC]
                    total = total + both * prof[j * LCH + i:j * LCH + i + 1]
            contrib[:, at] = total
            return c

        lax.fori_loop(0, PIX // TILE, gather, 0)
        owner = pix_ref[pl.ds(2, 1), :]
        slot = pix_ref[pl.ds(3, 1), :]
        want = (owner - owner // 2 * 2) * CY + slot
        slots = lax.broadcasted_iota(jnp.int32, (2 * CY, PIX), 0)
        hot = jnp.where(slots == want, 1.0, 0.0).astype(BF16)
        ch, cl = split(contrib[...])
        pair = owner // 2
        dims = (((1,), (1,)), ((), ()))

        def scatter(j, c):
            hs_, ls_ = [], []
            for i in range(8):
                mask = pair == j * 8 + i
                hs_.append(jnp.where(mask, ch, 0.0))
                ls_.append(jnp.where(mask, cl, 0.0))
            lh = jnp.concatenate(hs_, axis=0).astype(BF16)
            ll = jnp.concatenate(ls_, axis=0).astype(BF16)
            d = lax.dot_general(lh, hot, dims, preferred_element_type=F32)
            d = d + lax.dot_general(ll, hot, dims, preferred_element_type=F32)
            at = pl.ds(pl.multiple_of(j * 8 * SEC, 8 * SEC), 8 * SEC)
            dense_ref[0, at, :] = d[:, :CY]
            dense_ref[1, at, :] = d[:, CY:]
            return c

        lax.fori_loop(0, 8, scatter, 0)


def local(kap, adjoint, concentration, courant_x, courant_y, hx, hy, ker, kert, pix, wgt):
    def whole(a):
        return pl.BlockSpec(a.shape, lambda l, n=a.ndim: (0,) * n)

    field = pl.BlockSpec((SEC, 1, CX, CY), lambda l: (0, l, 0, 0))
    plane = pl.BlockSpec((1, CX, CY), lambda l: (l, 0, 0))
    return pl.pallas_call(
        local_kernel,
        grid=(LEV,),
        out_shape=(
            jax.ShapeDtypeStruct((SEC, LEV, CX, CY), F32),
            jax.ShapeDtypeStruct((2, 64 * SEC, CY), F32),
        ),
        in_specs=[
            whole(kap), field, field, plane, plane, whole(hx), whole(hy), whole(ker),
            whole(kert), whole(pix), whole(wgt),
        ],
        out_specs=(field, pl.BlockSpec((2, 64 * SEC, CY), lambda l: (0, 0, 0))),
        scratch_shapes=[
            pltpu.VMEM((LEV, 2 * SEC, CX * CY), BF16),
            pltpu.VMEM((SEC, PIX), F32),
        ],
        compiler_params=pltpu.CompilerParams(vmem_limit_bytes=56 << 20),
    )(kap, adjoint, concentration, courant_x, courant_y, hx, hy, ker, kert, pix, wgt)


def owners_kernel(d_ref, out_ref, d, rc, ra0, ra1, ra2, rb0, rb1, rb2, r20, r21, r22,
                  r30, r31, r32, ssem, rsem):
    x, y, z, c = place()

    def dev(axis, by):
        xx = lax.rem(x + by + 4, 4) if axis == 0 else x
        yy = lax.rem(y + by + 4, 4) if axis == 1 else y
        zz = lax.rem(z + by + 4, 4) if axis == 2 else z
        return (yy * 4 + xx, zz * 2 + c)

    sibling = (lax.axis_index("gx"), z * 2 + 1 - c)
    barrier = pltpu.get_barrier_semaphore()
    pl.semaphore_signal(barrier, 1, device_id=sibling, device_id_type=MESH)
    for axis in range(3):
        for by in (1, -1, 2):
            pl.semaphore_signal(barrier, 1, device_id=dev(axis, by), device_id_type=MESH)
    pl.semaphore_wait(barrier, 10)
    count = [0]

    def send(src, dst, peer):
        n = count[0]
        count[0] += 1
        copy = pltpu.make_async_remote_copy(
            src, dst, ssem.at[n], rsem.at[n], device_id=peer, device_id_type=MESH
        )
        copy.start()
        return copy

    mine = (x, y, z)

    def at(axis, by):
        return lax.rem(mine[axis] + by + 4, 4)

    def part(ref, band, fixed, lead=()):
        low, size = band
        idx = [slice(None)] * 3
        for axis, value in fixed.items():
            idx[(1, 0, 2)[axis]] = value
        return ref.at[tuple(lead) + tuple(idx) + (pl.ds(low, size),)]

    done = []
    first = send(d_ref.at[1 - c], rc, sibling)
    first.wait_recv()
    done.append(first)

    def total(i, carry):
        d[i // 4, lax.rem(i, 4)] = d_ref[c, i // 4, lax.rem(i, 4)] + rc[i // 4, lax.rem(i, 4)]
        return carry

    lax.fori_loop(0, 16, total, 0)
    ra, rb, r2, r3 = (ra0, ra1, ra2), (rb0, rb1, rb2), (r20, r21, r22), (r30, r31, r32)
    orders = ((0, 1, 2), (1, 2, 0), (2, 0, 1))
    step_a = []
    for g in range(3):
        a1 = orders[g][0]
        low, size = BANDS[g]
        half = size // 2 if size > 8 else 8
        ups = send(part(d, (low, half), {a1: at(a1, 2)}), ra[g].at[0], dev(a1, 1))
        downs = None
        if size > 8:
            downs = send(part(d, (low + half, half), {a1: at(a1, 2)}), ra[g].at[1], dev(a1, -1))
        step_a.append((ups, downs))
    step_b = []
    for g in range(3):
        a1 = orders[g][0]
        low, size = BANDS[g]
        half = size // 2 if size > 8 else 8
        ups, downs = step_a[g]
        ups.wait_recv()
        fwd = part(d, (low, half), {a1: at(a1, 1)})
        fwd[...] = fwd[...] + ra[g][0]
        if downs is not None:
            downs.wait_recv()
            fwd = part(d, (low + half, half), {a1: at(a1, -1)})
            fwd[...] = fwd[...] + ra[g][1]
        step_b.append((
            send(part(d, BANDS[g], {a1: at(a1, 1)}), rb[g].at[0], dev(a1, 1)),
            send(part(d, BANDS[g], {a1: at(a1, -1)}), rb[g].at[1], dev(a1, -1)),
        ))
        done.append(ups)
        if downs is not None:
            done.append(downs)
    step_2 = []
    for g in range(3):
        a1, a2, a3 = orders[g]
        for copy in step_b[g]:
            copy.wait_recv()
            done.append(copy)
        own = part(d, BANDS[g], {a1: mine[a1]})
        own[...] = own[...] + rb[g][0] + rb[g][1]
        step_2.append([
            send(part(d, BANDS[g], {a1: mine[a1], a2: at(a2, by)}), r2[g].at[i], dev(a2, by))
            for i, by in enumerate((1, -1, 2))
        ])
    step_3 = []
    for g in range(3):
        a1, a2, a3 = orders[g]
        for copy in step_2[g]:
            copy.wait_recv()
            done.append(copy)
        own = part(d, BANDS[g], {a1: mine[a1], a2: mine[a2]})
        own[...] = own[...] + r2[g][0] + r2[g][1] + r2[g][2]
        step_3.append([
            send(part(d, BANDS[g], {0: at(0, by if a3 == 0 else 0),
                                    1: at(1, by if a3 == 1 else 0),
                                    2: at(2, by if a3 == 2 else 0)}),
                 r3[g].at[i], dev(a3, by))
            for i, by in enumerate((1, -1, 2))
        ])
    for g in range(3):
        for copy in step_3[g]:
            copy.wait_recv()
            done.append(copy)
        low, size = BANDS[g]
        out_ref[pl.ds(low, size), :] = (
            d[y, x, z, pl.ds(low, size), :] + r3[g][0] + r3[g][1] + r3[g][2]
        )
    for copy in done:
        copy.wait_send()


def owners(dense):
    vmem = pl.BlockSpec(memory_space=pltpu.VMEM)

    def bands(*lead):
        return [pltpu.VMEM(tuple(lead) + (size, CY), F32) for _, size in BANDS]

    halves = [pltpu.VMEM((2, 4, 4, 8, CY), F32)] * 3
    return pl.pallas_call(
        owners_kernel,
        out_shape=jax.ShapeDtypeStruct((SEC, CY), F32),
        in_specs=[vmem],
        out_specs=vmem,
        scratch_shapes=[
            pltpu.VMEM((4, 4, 4, SEC, CY), F32),
            pltpu.VMEM((4, 4, 4, SEC, CY), F32),
            *halves,
            *bands(2, 4, 4),
            *bands(3, 4),
            *bands(3),
            pltpu.SemaphoreType.DMA((32,)),
            pltpu.SemaphoreType.DMA((32,)),
        ],
        compiler_params=pltpu.CompilerParams(
            collective_id=1, has_side_effects=True, vmem_limit_bytes=48 << 20
        ),
    )(dense)


def per_device(
    adjoint, concentration, courant_x, courant_y, diffusion, coag_kernel,
    pixel_column, pixel_owner, pixel_slot, pixel_level, pixel_weight,
):
    kap = jnp.broadcast_to(diffusion[:, None], (LEV, CY))
    pix = jnp.stack([pixel_column, pixel_level, pixel_owner[:, 0], pixel_slot])
    hx, hy = halos(kap, adjoint, courant_x, courant_y)
    out, dense = local(
        kap, adjoint, concentration, courant_x, courant_y, hx, hy, coag_kernel, coag_kernel.T,
        pix, pixel_weight[None, :],
    )
    return out, owners(dense.reshape(2, 4, 4, 4, SEC, CY))


def solution(mesh):
    pixels = P(("gx", "gy"))
    placed = (
        P(None, None, "gx", "gy"), P(None, None, "gx", "gy"), P(None, "gx", "gy"),
        P(None, "gx", "gy"), P(), P(), pixels, P(("gx", "gy"), None), pixels, pixels, pixels,
    )
    return jax.shard_map(
        per_device,
        mesh=mesh,
        in_specs=placed,
        out_specs=(P(None, None, "gx", "gy"), P(None, ("gx", "gy"))),
        check_vma=False,
    )
```

```python
import jax
import jax.numpy as jnp
from jax import lax
from jax.experimental import pallas as pl
from jax.experimental.pallas import tpu as pltpu
from jax.sharding import PartitionSpec as P

MESH = pl.DeviceIdType.MESH
F32 = jnp.float32
BF16 = jnp.bfloat16
SEC, LEV, CX, CY = 40, 16, 8, 128
PIX = 2048
LCH = 4
TILE = 256
BANDS = ((0, 16), (16, 16), (32, 8))


def split(v):
    hi = v.astype(BF16).astype(F32)
    return hi, v - hi


def place():
    gx = lax.axis_index("gx")
    gy = lax.axis_index("gy")
    return lax.rem(gx, 4), gx // 4, gy // 2, lax.rem(gy, 2)


EAST, WEST, NORTH, SOUTH, KEEP = range(5)
ORDERS = ((0, 1, 2), (1, 2, 0), (2, 0, 1))


def kernel(
    adj_h, conc_h, cx_h, cy_h, dif_ref, ker_h, col_h, own_h, slot_h, lev_h, wgt_h,
    out_ref, grad_ref,
    adj, conc, cx, cy, ker, col, own, slot, lev, wgt,
    coef, k3, k3t, px, py, rx, ry, cells, hot, prof, pairs, held0, held1, held2, contrib,
    d0, d1, d2, rc0, rc1, rc2, ra0, ra1, ra2, rb0, rb1, rb2, r20, r21, r22, r30, r31, r32,
    lsem, ssem, rsem,
):
    gx = lax.axis_index("gx")
    gy = lax.axis_index("gy")
    x, y, z, c = place()
    mine = (x, y, z)
    half_peers = (
        (lax.rem(gx + 15, 16), gy),
        (lax.rem(gx + 1, 16), gy),
        (gx, lax.rem(gy + 7, 8)),
        (gx, lax.rem(gy + 1, 8)),
    )

    def at(axis, by):
        return lax.rem(mine[axis] + by + 4, 4)

    def dev(axis, by):
        xx = at(0, by) if axis == 0 else x
        yy = at(1, by) if axis == 1 else y
        zz = at(2, by) if axis == 2 else z
        return (yy * 4 + xx, zz * 2 + c)

    sibling = (gx, z * 2 + 1 - c)
    barrier = pltpu.get_barrier_semaphore()
    for peer in half_peers:
        pl.semaphore_signal(barrier, 1, device_id=peer, device_id_type=MESH)
    pl.semaphore_signal(barrier, 1, device_id=sibling, device_id_type=MESH)
    for axis in range(3):
        for by in (1, -1, 2):
            pl.semaphore_signal(barrier, 1, device_id=dev(axis, by), device_id_type=MESH)
    loads = {}
    for i, (name, src, dst) in enumerate((
        ("cx", cx_h, cx), ("cy", cy_h, cy), ("adj", adj_h, adj), ("conc", conc_h, conc),
        ("ker", ker_h, ker), ("col", col_h, col), ("own", own_h, own), ("slot", slot_h, slot),
        ("lev", lev_h, lev), ("wgt", wgt_h, wgt),
    )):
        loads[name] = pltpu.make_async_copy(src, dst, lsem.at[i])
        loads[name].start()
    count = [0]
    done = []

    def send(src, dst, peer):
        n = count[0]
        count[0] += 1
        copy = pltpu.make_async_remote_copy(
            src, dst, ssem.at[n], rsem.at[n], device_id=peer, device_id_type=MESH
        )
        copy.start()
        done.append(copy)
        return copy

    loads["cx"].wait()
    loads["cy"].wait()

    def factors(l, carry):
        kap = dif_ref[l]
        a, b = cx[l], cy[l]
        coef[EAST, l] = jnp.maximum(a, 0.0) + kap
        coef[WEST, l] = jnp.maximum(-a, 0.0) + kap
        coef[NORTH, l] = jnp.maximum(b, 0.0) + kap
        coef[SOUTH, l] = jnp.maximum(-b, 0.0) + kap
        coef[KEEP, l] = 1.0 - jnp.abs(a) - jnp.abs(b) - 4.0 * kap
        return carry

    lax.fori_loop(0, LEV, factors, 0)
    loads["adj"].wait()
    first = coef[EAST, :, 0, :]
    last = coef[WEST, :, CX - 1, :]

    def fill(k, carry):
        px[0, k] = adj[k, :, 0, :] * first
        px[1, k] = adj[k, :, CX - 1, :] * last
        return carry

    lax.fori_loop(0, SEC, fill, 0)
    pl.semaphore_wait(barrier, 14)
    sent_x = [send(px.at[i], rx.at[i], half_peers[i]) for i in range(2)]
    lane = lax.broadcasted_iota(jnp.int32, (SEC, CY), 1)
    row = lax.broadcasted_iota(jnp.int32, (SEC, CY), 0)

    def edge(l, carry):
        low, high = carry
        for i in range(CX):
            a = adj[:, l, i, :]
            q = l * CX + i
            s = pltpu.roll(a * coef[NORTH, l, pl.ds(i, 1), :], q, 1)
            n = pltpu.roll(a * coef[SOUTH, l, pl.ds(i, 1), :], q + 1, 1)
            low = jnp.where(lane == q, s, low)
            high = jnp.where(lane == q, n, high)
        return low, high

    zero = jnp.zeros((SEC, CY), F32)
    low, high = lax.fori_loop(0, LEV, edge, (zero, zero))
    py[0] = low
    py[1] = high
    sent_y = [send(py.at[i], ry.at[i], half_peers[2 + i]) for i in range(2)]

    for name in ("ker", "col", "own", "slot", "lev", "wgt", "conc"):
        loads[name].wait()
    kh, kl = split(ker[...])
    k3[...] = jnp.concatenate([kh, kh, kl], axis=1).astype(BF16)
    kh, kl = split(ker[...].T)
    k3t[...] = jnp.concatenate([kh, kh, kl], axis=1).astype(BF16)
    height = lax.broadcasted_iota(jnp.int32, (LEV, PIX), 0).astype(F32) - lev[...].astype(F32)
    shape = jnp.exp(-height * height / 8.0)
    prof[...] = shape / jnp.sum(shape, axis=0, keepdims=True) * wgt[...]
    pair = own[...] // 2
    pairs[...] = jnp.broadcast_to(pair.astype(F32), (16, PIX)).astype(BF16)
    want = (own[...] - pair * 2) * CY + slot[...]

    def mark(i, carry):
        base = pl.multiple_of(i * 64, 64)
        ids = lax.broadcasted_iota(jnp.int32, (64, PIX), 0) + base
        cells[pl.ds(base, 64), :] = jnp.where(ids == col[...], 1.0, 0.0).astype(BF16)
        return carry

    lax.fori_loop(0, CX * CY // 64, mark, 0)
    for i in range(4):
        ids = lax.broadcasted_iota(jnp.int32, (64, PIX), 0) + i * 64
        hot[pl.ds(i * 64, 64), :] = jnp.where(ids == want, 1.0, 0.0).astype(BF16)

    def product(k, v):
        vh, vl = split(v)
        v3 = jnp.concatenate([vh, vl, vh], axis=0).astype(BF16)
        return jnp.dot(k[...], v3, preferred_element_type=F32)

    helds = (held0, held1, held2)
    far_e = jnp.where(gx == 15, 0.0, 1.0)
    far_w = jnp.where(gx == 0, 0.0, 1.0)
    far_n = jnp.where(gy == 7, 0.0, 1.0)
    far_s = jnp.where(gy == 0, 0.0, 1.0)

    def level(xs):
        def step(l, carry):
            turn = lax.rem(CY - l * CX, CY)
            hn = pltpu.roll(ry[0], turn, 1) * far_n
            hs = pltpu.roll(ry[1], turn, 1) * far_s

            def cf(kind, i):
                return coef[kind, l, pl.ds(i, 1), :]

            moved, ups, concs = [], [], []
            for i in xs:
                a = adj[:, l, i, :]
                m = cf(KEEP, i) * a
                if i < CX - 1:
                    m = m + cf(EAST, i + 1) * adj[:, l, i + 1, :]
                else:
                    m = m + rx[0, :, l, :] * far_e
                if i > 0:
                    m = m + cf(WEST, i - 1) * adj[:, l, i - 1, :]
                else:
                    m = m + rx[1, :, l, :] * far_w
                nh = pltpu.roll(hn, (CY - i) % CY, 1)
                sh = pltpu.roll(hs, (CY - 1 - i) % CY, 1)
                m = m + pltpu.roll(jnp.where(lane == 0, nh, cf(NORTH, i) * a), CY - 1, 1)
                m = m + pltpu.roll(jnp.where(lane == CY - 1, sh, cf(SOUTH, i) * a), 1, 1)
                nxt = jnp.where(row == SEC - 1, 0.0, pltpu.roll(m, SEC - 1, 0))
                moved.append(m)
                ups.append(nxt - m)
                concs.append(conc[:, l, i, :])
            m = jnp.concatenate(moved, axis=1)
            up = jnp.concatenate(ups, axis=1)
            cc = jnp.concatenate(concs, axis=1)
            res = m + up * product(k3, cc) + product(k3t, up * cc)
            rh, rl = split(res)
            for n, i in enumerate(xs):
                out_ref[:, l, i, :] = res[:, n * CY:(n + 1) * CY]
            for b, (start, size) in enumerate(BANDS):
                both = jnp.concatenate([rh[start:start + size], rl[start:start + size]], axis=0)
                both = both.astype(BF16)
                for n, i in enumerate(xs):
                    helds[b][l, :, i * CY:(i + 1) * CY] = both[:, n * CY:(n + 1) * CY]
            return carry

        lax.fori_loop(0, LEV, step, 0)

    for copy in sent_y:
        copy.wait_recv()
    level(range(1, CX - 1))
    for copy in sent_x:
        copy.wait_recv()
    level((0, CX - 1))

    ds, rc = (d0, d1, d2), (rc0, rc1, rc2)
    ra, rb, r2, r3 = (ra0, ra1, ra2), (rb0, rb1, rb2), (r20, r21, r22), (r30, r31, r32)

    def gather(b):
        size = BANDS[b][1]
        group = 256 // (2 * size)

        def tile(t, carry):
            where = pl.ds(pl.multiple_of(t * TILE, TILE), TILE)
            total = jnp.zeros((size, TILE), F32)
            for j in range(LEV // group):
                block = helds[b][pl.ds(j * group, group)].reshape(256, CX * CY)
                got = jnp.dot(block, cells[:, where], preferred_element_type=F32)
                for i in range(group):
                    base = i * 2 * size
                    both = got[base:base + size] + got[base + size:base + 2 * size]
                    total = total + both * prof[pl.ds(j * group + i, 1), where]
            contrib[pl.ds(0, size), where] = total
            return carry

        lax.fori_loop(0, PIX // TILE, tile, 0)

    dims = (((1,), (1,)), ((), ()))

    def scatter(b):
        size = BANDS[b][1]
        ch, cl = split(contrib[pl.ds(0, size), :])
        if size == 8:
            ch = jnp.concatenate([ch, cl], axis=0)
        ch = ch.astype(BF16)
        cl = cl.astype(BF16)
        none = jnp.zeros((16, PIX), BF16)
        copies = []
        for j in range(4):
            def rows(v):
                return jnp.concatenate(
                    [jnp.where(pairs[...] == float(j * 16 + i), v, none) for i in range(16)], axis=0
                )

            got = lax.dot_general(rows(ch), hot[...], dims, preferred_element_type=F32)
            if size == 16:
                got = got + lax.dot_general(rows(cl), hot[...], dims, preferred_element_type=F32)
                got = got.reshape(4, 4, 16, 2 * CY)
            else:
                got = got.reshape(4, 4, 16, 2 * CY)
                got = got[:, :, :8] + got[:, :, 8:]
            ds[b][0, j] = got[..., :CY]
            ds[b][1, j] = got[..., CY:]
            copies.append(send(ds[b].at[1 - c, j], rc[b].at[j], sibling))
        return copies

    def part(b, fixed, low, size):
        idx = [slice(None)] * 3
        for axis, value in fixed.items():
            idx[(1, 0, 2)[axis]] = value
        return ds[b].at[(c,) + tuple(idx) + (pl.ds(low, size),)]

    def stage_c(b, copies):
        for copy in copies:
            copy.wait_recv()

        def add(i, carry):
            j, k = i // 4, lax.rem(i, 4)
            ds[b][c, j, k] = ds[b][c, j, k] + rc[b][j, k]
            return carry

        lax.fori_loop(0, 16, add, 0)
        a1 = ORDERS[b][0]
        size = BANDS[b][1]
        out = [send(part(b, {a1: at(a1, 2)}, 0, 8), ra[b].at[0], dev(a1, 1))]
        if size > 8:
            out.append(send(part(b, {a1: at(a1, 2)}, 8, 8), ra[b].at[1], dev(a1, -1)))
        return out

    def stage_a(b, copies):
        a1 = ORDERS[b][0]
        for n, copy in enumerate(copies):
            copy.wait_recv()
            fwd = part(b, {a1: at(a1, (1, -1)[n])}, 8 * n, 8)
            fwd[...] = fwd[...] + ra[b][n]
        size = BANDS[b][1]
        return [
            send(part(b, {a1: at(a1, by)}, 0, size), rb[b].at[i], dev(a1, by))
            for i, by in enumerate((1, -1))
        ]

    def stage_b(b, copies):
        a1, a2, a3 = ORDERS[b]
        size = BANDS[b][1]
        for copy in copies:
            copy.wait_recv()
        here = part(b, {a1: mine[a1]}, 0, size)
        here[...] = here[...] + rb[b][0] + rb[b][1]
        return [
            send(part(b, {a1: mine[a1], a2: at(a2, by)}, 0, size), r2[b].at[i], dev(a2, by))
            for i, by in enumerate((1, -1, 2))
        ]

    def stage_2(b, copies):
        a1, a2, a3 = ORDERS[b]
        size = BANDS[b][1]
        for copy in copies:
            copy.wait_recv()
        here = part(b, {a1: mine[a1], a2: mine[a2]}, 0, size)
        here[...] = here[...] + r2[b][0] + r2[b][1] + r2[b][2]
        return [
            send(part(b, {n: at(n, by if n == a3 else 0) for n in range(3)}, 0, size),
                 r3[b].at[i], dev(a3, by))
            for i, by in enumerate((1, -1, 2))
        ]

    def stage_3(b, copies):
        start, size = BANDS[b]
        for copy in copies:
            copy.wait_recv()
        grad_ref[pl.ds(start, size), :] = ds[b][c, y, x, z] + r3[b][0] + r3[b][1] + r3[b][2]

    gather(0)
    a = scatter(0)
    gather(1)
    a = stage_c(0, a)
    b = scatter(1)
    a = stage_a(0, a)
    gather(2)
    b = stage_c(1, b)
    e = scatter(2)
    a = stage_b(0, a)
    b = stage_a(1, b)
    e = stage_c(2, e)
    a = stage_2(0, a)
    e = stage_a(2, e)
    b = stage_b(1, b)
    stage_3(0, a)
    e = stage_b(2, e)
    b = stage_2(1, b)
    e = stage_2(2, e)
    stage_3(1, b)
    stage_3(2, e)
    for copy in done:
        copy.wait_send()


def per_device(
    adjoint, concentration, courant_x, courant_y, diffusion, coag_kernel,
    pixel_column, pixel_owner, pixel_slot, pixel_level, pixel_weight,
):
    vmem = pl.BlockSpec(memory_space=pltpu.VMEM)
    smem = pl.BlockSpec(memory_space=pltpu.SMEM)
    hbm = pl.BlockSpec(memory_space=pltpu.HBM)
    field = (SEC, LEV, CX, CY)
    plane = (LEV, CX, CY)

    def bands(*lead):
        return [pltpu.VMEM(tuple(lead) + (size, CY), F32) for _, size in BANDS]

    ints = pltpu.VMEM((1, PIX), jnp.int32)
    return pl.pallas_call(
        kernel,
        out_shape=(
            jax.ShapeDtypeStruct(field, F32),
            jax.ShapeDtypeStruct((SEC, CY), F32),
        ),
        in_specs=[hbm, hbm, hbm, hbm, smem] + [hbm] * 6,
        out_specs=(vmem, vmem),
        scratch_shapes=[
            pltpu.VMEM(field, F32), pltpu.VMEM(field, F32),
            pltpu.VMEM(plane, F32), pltpu.VMEM(plane, F32),
            pltpu.VMEM((SEC, SEC), F32),
            ints, ints, ints, ints, pltpu.VMEM((1, PIX), F32),
            pltpu.VMEM((5,) + plane, F32),
            pltpu.VMEM((SEC, 3 * SEC), BF16), pltpu.VMEM((SEC, 3 * SEC), BF16),
            pltpu.VMEM((2, SEC, LEV, CY), F32), pltpu.VMEM((2, SEC, CY), F32),
            pltpu.VMEM((2, SEC, LEV, CY), F32), pltpu.VMEM((2, SEC, CY), F32),
            pltpu.VMEM((CX * CY, PIX), BF16), pltpu.VMEM((2 * CY, PIX), BF16),
            pltpu.VMEM((LEV, PIX), F32), pltpu.VMEM((16, PIX), BF16),
            *[pltpu.VMEM((LEV, 2 * size, CX * CY), BF16) for _, size in BANDS],
            pltpu.VMEM((16, PIX), F32),
            *bands(2, 4, 4, 4),
            *bands(4, 4, 4),
            *[pltpu.VMEM((size // 8, 4, 4, 8, CY), F32) for _, size in BANDS],
            *bands(2, 4, 4),
            *bands(3, 4),
            *bands(3),
            pltpu.SemaphoreType.DMA((10,)),
            pltpu.SemaphoreType.DMA((48,)),
            pltpu.SemaphoreType.DMA((48,)),
        ],
        compiler_params=pltpu.CompilerParams(
            collective_id=0, has_side_effects=True, vmem_limit_bytes=56 << 20
        ),
    )(
        adjoint, concentration, courant_x, courant_y, diffusion, coag_kernel,
        pixel_column[None, :], pixel_owner[:, 0][None, :], pixel_slot[None, :],
        pixel_level[None, :], pixel_weight[None, :],
    )


def solution(mesh):
    pixels = P(("gx", "gy"))
    placed = (
        P(None, None, "gx", "gy"), P(None, None, "gx", "gy"), P(None, "gx", "gy"),
        P(None, "gx", "gy"), P(), P(), pixels, P(("gx", "gy"), None), pixels, pixels, pixels,
    )
    return jax.shard_map(
        per_device,
        mesh=mesh,
        in_specs=placed,
        out_specs=(P(None, None, "gx", "gy"), P(None, ("gx", "gy"))),
        check_vma=False,
    )
```

```python
import jax
import jax.numpy as jnp
from jax import lax
from jax.experimental import pallas as pl
from jax.experimental.pallas import tpu as pltpu
from jax.sharding import PartitionSpec as P

MESH = pl.DeviceIdType.MESH
F32 = jnp.float32
BF16 = jnp.bfloat16
SEC, LEV, CX, CY = 40, 16, 8, 128
PIX = 2048
TILE = 1024
LCH = 4
BANDS = tuple((8 * b, 8) for b in range(5))
ORDERS = ((0, 1, 2), (1, 2, 0), (2, 0, 1), (0, 1, 2), (1, 2, 0))
GROUP_IN = 2
GROUP_OUT = 4
PLAN = (
    (0, 0), (1, 0), (0, 1), (2, 0), (1, 1), (3, 0), (2, 1), (4, 0),
    (0, 2), (3, 1), (4, 1), (1, 2), (0, 3), (2, 2), (1, 3), (3, 2), (2, 3), (0, 4), (4, 2),
    (1, 4), (3, 3), (2, 4), (4, 3), (3, 4), (4, 4),
)


def split(v):
    hi = v.astype(BF16).astype(F32)
    return hi, v - hi


def place():
    gx = lax.axis_index("gx")
    gy = lax.axis_index("gy")
    return lax.rem(gx, 4), gx // 4, gy // 2, lax.rem(gy, 2)


EAST, WEST, NORTH, SOUTH, KEEP = range(5)


def kernel(
    adj_h, conc_h, cx_h, cy_h, dif_ref, ker_h, col_h, own_h, slot_h, lev_h, wgt_h,
    out_ref, grad_ref,
    adj, conc, cx, cy, ker, col, own, slot, lev, wgt,
    coef, k3, k3t, px, py, rx, ry, cells, hot, prof, pairs, held, contrib, res,
    ds, rc, r1, r2, r3, lsem, osem, ssem, rsem,
):
    gx = lax.axis_index("gx")
    gy = lax.axis_index("gy")
    x, y, z, c = place()
    mine = (x, y, z)
    half_peers = (
        (lax.rem(gx + 15, 16), gy),
        (lax.rem(gx + 1, 16), gy),
        (gx, lax.rem(gy + 7, 8)),
        (gx, lax.rem(gy + 1, 8)),
    )

    def at(axis, by):
        return lax.rem(mine[axis] + by + 4, 4)

    def dev(axis, by):
        xx = at(0, by) if axis == 0 else x
        yy = at(1, by) if axis == 1 else y
        zz = at(2, by) if axis == 2 else z
        return (yy * 4 + xx, zz * 2 + c)

    sibling = (gx, z * 2 + 1 - c)
    barrier = pltpu.get_barrier_semaphore()
    for peer in half_peers:
        pl.semaphore_signal(barrier, 1, device_id=peer, device_id_type=MESH)
    pl.semaphore_signal(barrier, 1, device_id=sibling, device_id_type=MESH)
    for axis in range(3):
        for by in (1, -1, 2):
            pl.semaphore_signal(barrier, 1, device_id=dev(axis, by), device_id_type=MESH)
    loads = {}
    for i, (name, src, dst) in enumerate((
        ("cx", cx_h, cx), ("cy", cy_h, cy), ("adj", adj_h, adj), ("conc", conc_h, conc),
        ("ker", ker_h, ker), ("col", col_h, col), ("own", own_h, own), ("slot", slot_h, slot),
        ("lev", lev_h, lev), ("wgt", wgt_h, wgt),
    )):
        loads[name] = pltpu.make_async_copy(src, dst, lsem.at[i])
        loads[name].start()
    count = [0]
    done = []

    def send(src, dst, peer):
        n = count[0]
        count[0] += 1
        copy = pltpu.make_async_remote_copy(
            src, dst, ssem.at[n], rsem.at[n], device_id=peer, device_id_type=MESH
        )
        copy.start()
        done.append(copy)
        return copy

    loads["cx"].wait()
    loads["cy"].wait()

    def factors(l, carry):
        kap = dif_ref[l]
        a, b = cx[l], cy[l]
        coef[EAST, l] = jnp.maximum(a, 0.0) + kap
        coef[WEST, l] = jnp.maximum(-a, 0.0) + kap
        coef[NORTH, l] = jnp.maximum(b, 0.0) + kap
        coef[SOUTH, l] = jnp.maximum(-b, 0.0) + kap
        coef[KEEP, l] = 1.0 - jnp.abs(a) - jnp.abs(b) - 4.0 * kap
        return carry

    lax.fori_loop(0, LEV, factors, 0)
    loads["adj"].wait()
    first = coef[EAST, :, 0, :]
    last = coef[WEST, :, CX - 1, :]

    def fill(part):
        rows = slice(8 * part, 8 * part + 8)

        def one(k, carry):
            px[0, part, k] = adj[k, rows, 0, :] * first[rows]
            px[1, part, k] = adj[k, rows, CX - 1, :] * last[rows]
            return carry

        lax.fori_loop(0, SEC, one, 0, unroll=4)

    fill(0)
    pl.semaphore_wait(barrier, 14)
    sent_x = [[send(px.at[i, 0], rx.at[i, 0], half_peers[i]) for i in range(2)]]
    fill(1)
    sent_x.append([send(px.at[i, 1], rx.at[i, 1], half_peers[i]) for i in range(2)])
    lane = lax.broadcasted_iota(jnp.int32, (SEC, CY), 1)
    row = lax.broadcasted_iota(jnp.int32, (SEC, CY), 0)

    def edge(l, carry):
        low, high = carry
        for i in range(CX):
            a = adj[:, l, i, :]
            q = l * CX + i
            s = pltpu.roll(a * coef[NORTH, l, pl.ds(i, 1), :], q, 1)
            n = pltpu.roll(a * coef[SOUTH, l, pl.ds(i, 1), :], q + 1, 1)
            low = jnp.where(lane == q, s, low)
            high = jnp.where(lane == q, n, high)
        return low, high

    zero = jnp.zeros((SEC, CY), F32)
    low, high = lax.fori_loop(0, LEV, edge, (zero, zero))
    py[0] = low
    py[1] = high
    sent_y = [send(py.at[i], ry.at[i], half_peers[2 + i]) for i in range(2)]

    for name in ("ker", "col", "own", "slot", "lev", "wgt", "conc"):
        loads[name].wait()
    kh, kl = split(ker[...])
    k3[...] = jnp.concatenate([kh, kh, kl], axis=1).astype(BF16)
    kh, kl = split(ker[...].T)
    k3t[...] = jnp.concatenate([kh, kh, kl], axis=1).astype(BF16)
    height = lax.broadcasted_iota(jnp.int32, (LEV, PIX), 0).astype(F32) - lev[...].astype(F32)
    shape = jnp.exp(-height * height / 8.0)
    prof[...] = shape / jnp.sum(shape, axis=0, keepdims=True) * wgt[...]
    pair = own[...] // 2
    pairs[...] = jnp.broadcast_to(pair.astype(F32), (16, PIX)).astype(BF16)
    want = (own[...] - pair * 2) * CY + slot[...]

    turned = lax.rem(col[...] + (CX - 1) * CY, CX * CY)

    def mark(i, carry):
        base = pl.multiple_of(i * 64, 64)
        ids = lax.broadcasted_iota(jnp.int32, (64, PIX), 0) + base
        cells[pl.ds(base, 64), :] = jnp.where(ids == turned, 1.0, 0.0).astype(BF16)
        return carry

    lax.fori_loop(0, CX * CY // 64, mark, 0)
    for i in range(4):
        ids = lax.broadcasted_iota(jnp.int32, (64, PIX), 0) + i * 64
        hot[pl.ds(i * 64, 64), :] = jnp.where(ids == want, 1.0, 0.0).astype(BF16)

    def product(k, v):
        vh, vl = split(v)
        v3 = jnp.concatenate([vh, vl, vh], axis=0).astype(BF16)
        return jnp.dot(k[...], v3, preferred_element_type=F32)

    far_e = jnp.where(gx == 15, 0.0, 1.0)
    far_w = jnp.where(gx == 0, 0.0, 1.0)
    far_n = jnp.where(gy == 7, 0.0, 1.0)
    far_s = jnp.where(gy == 0, 0.0, 1.0)

    def levels(xs, group, start, stop):
        def step(it, carry):
            moved, ups, concs = [], [], []
            for g in range(group):
                l = it * group + g
                turn = lax.rem(CY - l * CX, CY)
                hn = pltpu.roll(ry[0], turn, 1) * far_n
                hs = pltpu.roll(ry[1], turn, 1) * far_s

                def cf(kind, i):
                    return coef[kind, l, pl.ds(i, 1), :]

                for i in xs:
                    a = adj[:, l, i, :]
                    m = cf(KEEP, i) * a
                    if i < CX - 1:
                        m = m + cf(EAST, i + 1) * adj[:, l, i + 1, :]
                    else:
                        m = m + rx[0, l // 8, :, lax.rem(l, 8), :] * far_e
                    if i > 0:
                        m = m + cf(WEST, i - 1) * adj[:, l, i - 1, :]
                    else:
                        m = m + rx[1, l // 8, :, lax.rem(l, 8), :] * far_w
                    nh = pltpu.roll(hn, (CY - i) % CY, 1)
                    sh = pltpu.roll(hs, (CY - 1 - i) % CY, 1)
                    m = m + pltpu.roll(jnp.where(lane == 0, nh, cf(NORTH, i) * a), CY - 1, 1)
                    m = m + pltpu.roll(jnp.where(lane == CY - 1, sh, cf(SOUTH, i) * a), 1, 1)
                    nxt = jnp.where(row == SEC - 1, 0.0, pltpu.roll(m, SEC - 1, 0))
                    moved.append(m)
                    ups.append(nxt - m)
                    concs.append(conc[:, l, i, :])
            m = jnp.concatenate(moved, axis=1)
            up = jnp.concatenate(ups, axis=1)
            cc = jnp.concatenate(concs, axis=1)
            new = m + up * product(k3, cc) + product(k3t, up * cc)
            rh, rl = split(new)
            both = jnp.concatenate([rh, rl], axis=0).astype(BF16)
            n = 0
            for g in range(group):
                l = it * group + g
                at_row = pl.ds(pl.multiple_of(l * 2 * SEC, 2 * SEC), 2 * SEC)
                for i in xs:
                    lanes = slice(n * CY, (n + 1) * CY)
                    spot = (i + CX - 1) % CX * CY
                    res[:, l, i, :] = new[:, lanes]
                    held[at_row, spot:spot + CY] = both[:, lanes]
                    n += 1
            return carry

        lax.fori_loop(start, stop, step, 0)

    def gather(low, high, more):
        def tile(t, carry):
            where = pl.ds(pl.multiple_of(t * TILE, TILE), TILE)
            total = contrib[:, where] if more else jnp.zeros((SEC, TILE), F32)
            onehot = cells[low:high, where]
            for j in range(0, LEV, LCH):
                block = held[j * 2 * SEC:(j + LCH) * 2 * SEC, low:high]
                got = jnp.dot(block, onehot, preferred_element_type=F32)
                for l in range(LCH):
                    base = l * 2 * SEC
                    both = got[base:base + SEC] + got[base + SEC:base + 2 * SEC]
                    total = total + both * prof[pl.ds(j + l, 1), where]
            contrib[:, where] = total
            return carry

        lax.fori_loop(0, PIX // TILE, tile, 0)

    for copy in sent_y:
        copy.wait_recv()
    levels(range(1, CX - 1), GROUP_IN, 0, LEV // GROUP_IN)
    gather(0, 6 * CY, False)
    for n in range(2):
        for copy in sent_x[n]:
            copy.wait_recv()
        levels((CX - 1, 0), GROUP_OUT, n * 8 // GROUP_OUT, (n + 1) * 8 // GROUP_OUT)
    out = pltpu.make_async_copy(res, out_ref, osem)
    out.start()
    gather(6 * CY, 8 * CY, True)

    dims = (((1,), (1,)), ((), ()))

    def scatter(b):
        low, size = BANDS[b]
        ch, cl = split(contrib[pl.ds(low, size), :])
        both = jnp.concatenate([ch, cl], axis=0).astype(BF16)
        none = jnp.zeros((16, PIX), BF16)
        copies = []
        for j in range(4):
            rows = jnp.concatenate(
                [jnp.where(pairs[...] == float(j * 16 + i), both, none) for i in range(16)], axis=0
            )
            got = lax.dot_general(rows, hot[...], dims, preferred_element_type=F32)
            got = got.reshape(4, 4, 16, 2 * CY)
            got = got[:, :, :8] + got[:, :, 8:]
            ds[b, 0, j] = got[..., :CY]
            ds[b, 1, j] = got[..., CY:]
            if j % 2:
                two = pl.ds(j - 1, 2)
                copies.append(send(ds.at[b, 1 - c, two], rc.at[b, two], sibling))
        return copies

    def part(b, fixed):
        idx = [slice(None)] * 3
        for axis, value in fixed.items():
            idx[(1, 0, 2)[axis]] = value
        return ds.at[(b, c) + tuple(idx)]

    sides = ((0, 1), (1, -1), (2, 2))

    def stage_c(b, copies):
        for copy in copies:
            copy.wait_recv()

        def add(i, carry):
            ds[b, c, i] = ds[b, c, i] + rc[b, i]
            return carry

        lax.fori_loop(0, 4, add, 0)
        a1 = ORDERS[b][0]
        return [send(part(b, {a1: at(a1, by)}), r1.at[b, i], dev(a1, by)) for i, by in sides]

    def stage_1(b, copies):
        a1, a2, a3 = ORDERS[b]
        for copy in copies:
            copy.wait_recv()
        here = part(b, {a1: mine[a1]})
        here[...] = here[...] + r1[b, 0] + r1[b, 1] + r1[b, 2]
        return [
            send(part(b, {a1: mine[a1], a2: at(a2, by)}), r2.at[b, i], dev(a2, by))
            for i, by in sides
        ]

    def stage_2(b, copies):
        a1, a2, a3 = ORDERS[b]
        for copy in copies:
            copy.wait_recv()
        here = part(b, {a1: mine[a1], a2: mine[a2]})
        here[...] = here[...] + r2[b, 0] + r2[b, 1] + r2[b, 2]
        return [
            send(part(b, {n: at(n, by if n == a3 else 0) for n in range(3)}),
                 r3.at[b, i], dev(a3, by))
            for i, by in sides
        ]

    def stage_3(b, copies):
        start, size = BANDS[b]
        for copy in copies:
            copy.wait_recv()
        grad_ref[pl.ds(start, size), :] = ds[b, c, y, x, z] + r3[b, 0] + r3[b, 1] + r3[b, 2]

    stages = (scatter, stage_c, stage_1, stage_2, stage_3)
    work = {}
    for b, n in PLAN:
        work[b] = stages[n](b, work[b]) if n else scatter(b)
    out.wait()
    for copy in done:
        copy.wait_send()


def per_device(
    adjoint, concentration, courant_x, courant_y, diffusion, coag_kernel,
    pixel_column, pixel_owner, pixel_slot, pixel_level, pixel_weight,
):
    vmem = pl.BlockSpec(memory_space=pltpu.VMEM)
    smem = pl.BlockSpec(memory_space=pltpu.SMEM)
    hbm = pl.BlockSpec(memory_space=pltpu.HBM)
    field = (SEC, LEV, CX, CY)
    plane = (LEV, CX, CY)

    ints = pltpu.VMEM((1, PIX), jnp.int32)
    return pl.pallas_call(
        kernel,
        out_shape=(
            jax.ShapeDtypeStruct(field, F32),
            jax.ShapeDtypeStruct((SEC, CY), F32),
        ),
        in_specs=[hbm, hbm, hbm, hbm, smem] + [hbm] * 6,
        out_specs=(hbm, vmem),
        scratch_shapes=[
            pltpu.VMEM(field, F32), pltpu.VMEM(field, F32),
            pltpu.VMEM(plane, F32), pltpu.VMEM(plane, F32),
            pltpu.VMEM((SEC, SEC), F32),
            ints, ints, ints, ints, pltpu.VMEM((1, PIX), F32),
            pltpu.VMEM((5,) + plane, F32),
            pltpu.VMEM((SEC, 3 * SEC), BF16), pltpu.VMEM((SEC, 3 * SEC), BF16),
            pltpu.VMEM((2, 2, SEC, 8, CY), F32), pltpu.VMEM((2, SEC, CY), F32),
            pltpu.VMEM((2, 2, SEC, 8, CY), F32), pltpu.VMEM((2, SEC, CY), F32),
            pltpu.VMEM((CX * CY, PIX), BF16), pltpu.VMEM((2 * CY, PIX), BF16),
            pltpu.VMEM((LEV, PIX), F32), pltpu.VMEM((16, PIX), BF16),
            pltpu.VMEM((LEV * 2 * SEC, CX * CY), BF16),
            pltpu.VMEM((SEC, PIX), F32),
            pltpu.VMEM(field, F32),
            pltpu.VMEM((5, 2, 4, 4, 4, 8, CY), F32),
            pltpu.VMEM((5, 4, 4, 4, 8, CY), F32),
            pltpu.VMEM((5, 3, 4, 4, 8, CY), F32),
            pltpu.VMEM((5, 3, 4, 8, CY), F32),
            pltpu.VMEM((5, 3, 8, CY), F32),
            pltpu.SemaphoreType.DMA((10,)),
            pltpu.SemaphoreType.DMA,
            pltpu.SemaphoreType.DMA((61,)),
            pltpu.SemaphoreType.DMA((61,)),
        ],
        compiler_params=pltpu.CompilerParams(
            collective_id=0, has_side_effects=True, vmem_limit_bytes=56 << 20
        ),
    )(
        adjoint, concentration, courant_x, courant_y, diffusion, coag_kernel,
        pixel_column[None, :], pixel_owner[:, 0][None, :], pixel_slot[None, :],
        pixel_level[None, :], pixel_weight[None, :],
    )


def solution(mesh):
    pixels = P(("gx", "gy"))
    placed = (
        P(None, None, "gx", "gy"), P(None, None, "gx", "gy"), P(None, "gx", "gy"),
        P(None, "gx", "gy"), P(), P(), pixels, P(("gx", "gy"), None), pixels, pixels, pixels,
    )
    return jax.shard_map(
        per_device,
        mesh=mesh,
        in_specs=placed,
        out_specs=(P(None, None, "gx", "gy"), P(None, ("gx", "gy"))),
        check_vma=False,
    )
```

```python
import jax
import jax.numpy as jnp
from jax import lax
from jax.experimental import pallas as pl
from jax.experimental.pallas import tpu as pltpu
from jax.sharding import PartitionSpec as P

MESH = pl.DeviceIdType.MESH
F32 = jnp.float32
BF16 = jnp.bfloat16
SEC, LEV, CX, CY = 40, 16, 8, 128
PIX = 2048
TILE = 1024
LCH = 4
BANDS = tuple((8 * b, 8) for b in range(5))
ORDERS = ((0, 1, 2), (1, 2, 0), (2, 0, 1), (0, 1, 2), (1, 2, 0))
GROUP_IN = 2
GROUP_OUT = 4
PLAN = (
    (0, 2), (1, 2), (2, 2), (0, 3), (3, 2), (1, 3), (4, 2), (2, 3), (0, 4), (3, 3), (1, 4),
    (4, 3), (2, 4), (3, 4), (4, 4),
)


def split(v):
    hi = v.astype(BF16).astype(F32)
    return hi, v - hi


def place():
    gx = lax.axis_index("gx")
    gy = lax.axis_index("gy")
    return lax.rem(gx, 4), gx // 4, gy // 2, lax.rem(gy, 2)


EAST, WEST, NORTH, SOUTH, KEEP = range(5)


def kernel(
    adj_h, conc_h, cx_h, cy_h, dif_ref, ker_h, col_h, own_h, slot_h, lev_h, wgt_h,
    out_ref, grad_ref,
    adj, conc, cx, cy, ker, col, own, slot, lev, wgt,
    coef, k3, k3t, rates, px, py, rx, ry, cells, hot, prof, pairs, held, contrib, contrib2, own2, slot2, pairs2, hot2,
    ds, r1, r2, r3, lsem, ssem, rsem,
):
    gx = lax.axis_index("gx")
    gy = lax.axis_index("gy")
    x, y, z, c = place()
    mine = (x, y, z)
    half_peers = (
        (lax.rem(gx + 15, 16), gy),
        (lax.rem(gx + 1, 16), gy),
        (gx, lax.rem(gy + 7, 8)),
        (gx, lax.rem(gy + 1, 8)),
    )

    def at(axis, by):
        return lax.rem(mine[axis] + by + 4, 4)

    def dev(axis, by):
        xx = at(0, by) if axis == 0 else x
        yy = at(1, by) if axis == 1 else y
        zz = at(2, by) if axis == 2 else z
        return (yy * 4 + xx, zz * 2 + c)

    sibling = (gx, z * 2 + 1 - c)
    barrier = pltpu.get_barrier_semaphore()
    for peer in half_peers:
        pl.semaphore_signal(barrier, 1, device_id=peer, device_id_type=MESH)
    pl.semaphore_signal(barrier, 1, device_id=sibling, device_id_type=MESH)
    for axis in range(3):
        for by in (1, -1, 2):
            pl.semaphore_signal(barrier, 1, device_id=dev(axis, by), device_id_type=MESH)
    loads = {}
    for i, (name, src, dst) in enumerate((
        ("cx", cx_h, cx), ("cy", cy_h, cy), ("adj", adj_h, adj), ("conc", conc_h, conc),
        ("ker", ker_h, ker), ("col", col_h, col), ("own", own_h, own), ("slot", slot_h, slot),
        ("lev", lev_h, lev), ("wgt", wgt_h, wgt),
    )):
        loads[name] = pltpu.make_async_copy(src, dst, lsem.at[i])
        loads[name].start()
    count = [0]
    done = []

    def send(src, dst, peer):
        n = count[0]
        count[0] += 1
        copy = pltpu.make_async_remote_copy(
            src, dst, ssem.at[n], rsem.at[n], device_id=peer, device_id_type=MESH
        )
        copy.start()
        done.append(copy)
        return copy

    loads["cx"].wait()
    loads["cy"].wait()

    def factors(l, carry):
        kap = dif_ref[l]
        a, b = cx[l], cy[l]
        coef[EAST, l] = jnp.maximum(a, 0.0) + kap
        coef[WEST, l] = jnp.maximum(-a, 0.0) + kap
        coef[NORTH, l] = jnp.maximum(b, 0.0) + kap
        coef[SOUTH, l] = jnp.maximum(-b, 0.0) + kap
        coef[KEEP, l] = 1.0 - jnp.abs(a) - jnp.abs(b) - 4.0 * kap
        return carry

    lax.fori_loop(0, LEV, factors, 0)
    loads["adj"].wait()
    first = coef[EAST, :, 0, :]
    last = coef[WEST, :, CX - 1, :]

    def fill(part):
        rows = slice(8 * part, 8 * part + 8)

        def one(k, carry):
            px[0, part, k] = adj[k, rows, 0, :] * first[rows]
            px[1, part, k] = adj[k, rows, CX - 1, :] * last[rows]
            return carry

        lax.fori_loop(0, SEC, one, 0, unroll=4)

    fill(0)
    pl.semaphore_wait(barrier, 14)
    sent_x = [[send(px.at[i, 0], rx.at[i, 0], half_peers[i]) for i in range(2)]]
    lane = lax.broadcasted_iota(jnp.int32, (SEC, CY), 1)
    row = lax.broadcasted_iota(jnp.int32, (SEC, CY), 0)

    def edge(l, carry):
        low, high = carry
        for i in range(CX):
            a = adj[:, l, i, :]
            q = l * CX + i
            s = pltpu.roll(a * coef[NORTH, l, pl.ds(i, 1), :], q, 1)
            n = pltpu.roll(a * coef[SOUTH, l, pl.ds(i, 1), :], q + 1, 1)
            low = jnp.where(lane == q, s, low)
            high = jnp.where(lane == q, n, high)
        return low, high

    zero = jnp.zeros((SEC, CY), F32)
    low, high = lax.fori_loop(0, LEV, edge, (zero, zero))
    py[0] = low
    py[1] = high

    sent_y = [send(py.at[i], ry.at[i], half_peers[2 + i]) for i in range(2)]
    fill(1)
    sent_x.append([send(px.at[i, 1], rx.at[i, 1], half_peers[i]) for i in range(2)])
    loads["own"].wait()
    loads["slot"].wait()
    sent_i = [send(own, own2, sibling), send(slot, slot2, sibling)]

    loads["ker"].wait()
    loads["conc"].wait()
    kh, kl = split(ker[...])
    k3[...] = jnp.concatenate([kh, kh, kl], axis=1).astype(BF16)
    kh, kl = split(ker[...].T)
    k3t[...] = jnp.concatenate([kh, kh, kl], axis=1).astype(BF16)
    def product(k, v):
        vh, vl = split(v)
        v3 = jnp.concatenate([vh, vl, vh], axis=0).astype(BF16)
        return jnp.dot(k[...], v3, preferred_element_type=F32)

    def rate(it, carry):
        cc = jnp.concatenate(
            [conc[:, it * 2 + g, i, :] for g in range(2) for i in range(CX)], axis=1
        )
        got = product(k3, cc)
        for g in range(2):
            base = pl.multiple_of((it * 2 + g) * SEC, SEC)
            rates[pl.ds(base, SEC), :] = got[:, g * CX * CY:(g + 1) * CX * CY]
        return carry

    lax.fori_loop(0, LEV // 2, rate, 0)
    for name in ("col", "lev", "wgt"):
        loads[name].wait()
    height = lax.broadcasted_iota(jnp.int32, (LEV, PIX), 0).astype(F32) - lev[...].astype(F32)
    shape = jnp.exp(-height * height / 8.0)
    prof[...] = shape / jnp.sum(shape, axis=0, keepdims=True) * wgt[...]
    def targets(owner, place_in, pair_out, hot_out):
        cell = owner[...] // 2
        pair_out[...] = jnp.broadcast_to((cell // 2).astype(F32), (16, PIX)).astype(BF16)
        want = (cell - cell // 2 * 2) * CY + place_in[...]
        want = jnp.where(owner[...] - cell * 2 == c, want, -1)
        for i in range(4):
            ids = lax.broadcasted_iota(jnp.int32, (64, PIX), 0) + i * 64
            hot_out[pl.ds(i * 64, 64), :] = jnp.where(ids == want, 1.0, 0.0).astype(BF16)

    targets(own, slot, pairs, hot)
    turned = lax.rem(col[...] + (CX - 1) * CY, CX * CY)

    def mark(i, carry):
        base = pl.multiple_of(i * 64, 64)
        ids = lax.broadcasted_iota(jnp.int32, (64, PIX), 0) + base
        cells[pl.ds(base, 64), :] = jnp.where(ids == turned, 1.0, 0.0).astype(BF16)
        return carry

    lax.fori_loop(0, CX * CY // 64, mark, 0)

    far_e = jnp.where(gx == 15, 0.0, 1.0)
    far_w = jnp.where(gx == 0, 0.0, 1.0)
    far_n = jnp.where(gy == 7, 0.0, 1.0)
    far_s = jnp.where(gy == 0, 0.0, 1.0)

    def levels(xs, group, start, stop):
        def step(it, carry):
            moved, ups, concs, turns = [], [], [], []
            for g in range(group):
                l = it * group + g
                turn = lax.rem(CY - l * CX, CY)
                hn = pltpu.roll(ry[0], turn, 1) * far_n
                hs = pltpu.roll(ry[1], turn, 1) * far_s

                def cf(kind, i):
                    return coef[kind, l, pl.ds(i, 1), :]

                for i in xs:
                    a = adj[:, l, i, :]
                    m = cf(KEEP, i) * a
                    if i < CX - 1:
                        m = m + cf(EAST, i + 1) * adj[:, l, i + 1, :]
                    else:
                        m = m + rx[0, l // 8, :, lax.rem(l, 8), :] * far_e
                    if i > 0:
                        m = m + cf(WEST, i - 1) * adj[:, l, i - 1, :]
                    else:
                        m = m + rx[1, l // 8, :, lax.rem(l, 8), :] * far_w
                    nh = pltpu.roll(hn, (CY - i) % CY, 1)
                    sh = pltpu.roll(hs, (CY - 1 - i) % CY, 1)
                    m = m + pltpu.roll(jnp.where(lane == 0, nh, cf(NORTH, i) * a), CY - 1, 1)
                    m = m + pltpu.roll(jnp.where(lane == CY - 1, sh, cf(SOUTH, i) * a), 1, 1)
                    nxt = jnp.where(row == SEC - 1, 0.0, pltpu.roll(m, SEC - 1, 0))
                    moved.append(m)
                    ups.append(nxt - m)
                    concs.append(conc[:, l, i, :])
                    base = pl.multiple_of(l * SEC, SEC)
                    turns.append(rates[pl.ds(base, SEC), i * CY:(i + 1) * CY])
            m = jnp.concatenate(moved, axis=1)
            up = jnp.concatenate(ups, axis=1)
            cc = jnp.concatenate(concs, axis=1)
            new = m + up * jnp.concatenate(turns, axis=1) + product(k3t, up * cc)
            rh, rl = split(new)
            both = jnp.concatenate([rh, rl], axis=0).astype(BF16)
            n = 0
            for g in range(group):
                l = it * group + g
                at_row = pl.ds(pl.multiple_of(l * 2 * SEC, 2 * SEC), 2 * SEC)
                for i in xs:
                    lanes = slice(n * CY, (n + 1) * CY)
                    spot = (i + CX - 1) % CX * CY
                    out_ref[:, l, i, :] = new[:, lanes]
                    held[at_row, spot:spot + CY] = both[:, lanes]
                    n += 1
            return carry

        lax.fori_loop(start, stop, step, 0)

    def gather(low, high, more):
        def tile(t, carry):
            where = pl.ds(pl.multiple_of(t * TILE, TILE), TILE)
            total = contrib[:, where] if more else jnp.zeros((SEC, TILE), F32)
            onehot = cells[low:high, where]
            for j in range(0, LEV, LCH):
                block = held[j * 2 * SEC:(j + LCH) * 2 * SEC, low:high]
                got = jnp.dot(block, onehot, preferred_element_type=F32)
                for l in range(LCH):
                    base = l * 2 * SEC
                    both = got[base:base + SEC] + got[base + SEC:base + 2 * SEC]
                    total = total + both * prof[pl.ds(j + l, 1), where]
            contrib[:, where] = total
            return carry

        lax.fori_loop(0, PIX // TILE, tile, 0)

    for copy in sent_y:
        copy.wait_recv()
    levels(range(1, CX - 1), GROUP_IN, 0, LEV // GROUP_IN)
    gather(0, 6 * CY, False)
    for copy in sent_i:
        copy.wait_recv()
    targets(own2, slot2, pairs2, hot2)
    for n in range(2):
        for copy in sent_x[n]:
            copy.wait_recv()
        levels((CX - 1, 0), GROUP_OUT, n * 8 // GROUP_OUT, (n + 1) * 8 // GROUP_OUT)
    gather(6 * CY, 8 * CY, True)
    swap = send(contrib, contrib2, sibling)

    dims = (((1,), (1,)), ((), ()))

    def scatter(b, values, pair_in, hot_in, more):
        low, size = BANDS[b]
        ch, cl = split(values[pl.ds(low, size), :])
        both = jnp.concatenate([ch, cl], axis=0).astype(BF16)
        none = jnp.zeros((16, PIX), BF16)
        for j in range(2):
            rows = jnp.concatenate(
                [jnp.where(pair_in[...] == float(j * 16 + i), both, none) for i in range(16)],
                axis=0,
            )
            got = lax.dot_general(rows, hot_in[...], dims, preferred_element_type=F32)
            for i in range(16):
                yy, xx, zz = j * 2 + i // 8, i // 2 % 4, i % 2 * 2
                one = got[i * 16:i * 16 + 8] + got[i * 16 + 8:i * 16 + 16]
                for k in range(2):
                    new = one[:, k * CY:(k + 1) * CY]
                    if more:
                        new = new + ds[b, yy, xx, zz + k]
                    ds[b, yy, xx, zz + k] = new

    def part(b, fixed):
        idx = [slice(None)] * 3
        for axis, value in fixed.items():
            idx[(1, 0, 2)[axis]] = value
        return ds.at[(b,) + tuple(idx)]

    sides = ((0, 1), (1, -1), (2, 2))

    def stage_c(b):
        scatter(b, contrib2, pairs2, hot2, True)
        a1 = ORDERS[b][0]
        return [send(part(b, {a1: at(a1, by)}), r1.at[b, i], dev(a1, by)) for i, by in sides]

    def stage_1(b, copies):
        a1, a2, a3 = ORDERS[b]
        for copy in copies:
            copy.wait_recv()
        here = part(b, {a1: mine[a1]})
        here[...] = here[...] + r1[b, 0] + r1[b, 1] + r1[b, 2]
        return [
            send(part(b, {a1: mine[a1], a2: at(a2, by)}), r2.at[b, i], dev(a2, by))
            for i, by in sides
        ]

    def stage_2(b, copies):
        a1, a2, a3 = ORDERS[b]
        for copy in copies:
            copy.wait_recv()
        here = part(b, {a1: mine[a1], a2: mine[a2]})
        here[...] = here[...] + r2[b, 0] + r2[b, 1] + r2[b, 2]
        return [
            send(part(b, {n: at(n, by if n == a3 else 0) for n in range(3)}),
                 r3.at[b, i], dev(a3, by))
            for i, by in sides
        ]

    def stage_3(b, copies):
        start, size = BANDS[b]
        for copy in copies:
            copy.wait_recv()
        grad_ref[pl.ds(start, size), :] = ds[b, y, x, z] + r3[b, 0] + r3[b, 1] + r3[b, 2]

    for b in range(5):
        scatter(b, contrib, pairs, hot, False)
    swap.wait_recv()
    stages = (None, None, stage_1, stage_2, stage_3)
    work = [stage_c(b) for b in range(5)]
    for b, n in PLAN:
        work[b] = stages[n](b, work[b])
    for copy in done:
        copy.wait_send()


def store_kernel(src, grad, dst, grad_dst, sems):
    copies = [
        pltpu.make_async_copy(src.at[pl.ds(5 * n, 5)], dst.at[pl.ds(5 * n, 5)], sems.at[n])
        for n in range(8)
    ]
    copies.append(pltpu.make_async_copy(grad, grad_dst, sems.at[8]))
    for copy in copies:
        copy.start()
    for copy in copies:
        copy.wait()


def per_device(
    adjoint, concentration, courant_x, courant_y, diffusion, coag_kernel,
    pixel_column, pixel_owner, pixel_slot, pixel_level, pixel_weight,
):
    vmem = pl.BlockSpec(memory_space=pltpu.VMEM)
    smem = pl.BlockSpec(memory_space=pltpu.SMEM)
    hbm = pl.BlockSpec(memory_space=pltpu.HBM)
    field = (SEC, LEV, CX, CY)
    plane = (LEV, CX, CY)

    ints = pltpu.VMEM((1, PIX), jnp.int32)
    got, grad = pl.pallas_call(
        kernel,
        out_shape=(
            jax.ShapeDtypeStruct(field, F32),
            jax.ShapeDtypeStruct((SEC, CY), F32),
        ),
        in_specs=[hbm, hbm, hbm, hbm, smem] + [hbm] * 6,
        out_specs=(vmem, vmem),
        scratch_shapes=[
            pltpu.VMEM(field, F32), pltpu.VMEM(field, F32),
            pltpu.VMEM(plane, F32), pltpu.VMEM(plane, F32),
            pltpu.VMEM((SEC, SEC), F32),
            ints, ints, ints, ints, pltpu.VMEM((1, PIX), F32),
            pltpu.VMEM((5,) + plane, F32),
            pltpu.VMEM((SEC, 3 * SEC), BF16), pltpu.VMEM((SEC, 3 * SEC), BF16),
            pltpu.VMEM((LEV * SEC, CX * CY), F32),
            pltpu.VMEM((2, 2, SEC, 8, CY), F32), pltpu.VMEM((2, SEC, CY), F32),
            pltpu.VMEM((2, 2, SEC, 8, CY), F32), pltpu.VMEM((2, SEC, CY), F32),
            pltpu.VMEM((CX * CY, PIX), BF16), pltpu.VMEM((2 * CY, PIX), BF16),
            pltpu.VMEM((LEV, PIX), F32), pltpu.VMEM((16, PIX), BF16),
            pltpu.VMEM((LEV * 2 * SEC, CX * CY), BF16),
            pltpu.VMEM((SEC, PIX), F32), pltpu.VMEM((SEC, PIX), F32),
            ints, ints, pltpu.VMEM((16, PIX), BF16), pltpu.VMEM((2 * CY, PIX), BF16),
            pltpu.VMEM((5, 4, 4, 4, 8, CY), F32),
            pltpu.VMEM((5, 3, 4, 4, 8, CY), F32),
            pltpu.VMEM((5, 3, 4, 8, CY), F32),
            pltpu.VMEM((5, 3, 8, CY), F32),
            pltpu.SemaphoreType.DMA((10,)),
            pltpu.SemaphoreType.DMA((54,)),
            pltpu.SemaphoreType.DMA((54,)),
        ],
        compiler_params=pltpu.CompilerParams(
            collective_id=0, has_side_effects=True, vmem_limit_bytes=48 << 20
        ),
    )(*(pltpu.with_memory_space_constraint(v, pltpu.HBM) for v in (
        adjoint, concentration, courant_x, courant_y, diffusion, coag_kernel,
        pixel_column[None, :], pixel_owner[:, 0][None, :], pixel_slot[None, :],
        pixel_level[None, :], pixel_weight[None, :],
    )))
    return pl.pallas_call(
        store_kernel,
        out_shape=(
            jax.ShapeDtypeStruct(field, F32),
            jax.ShapeDtypeStruct((SEC, CY), F32),
        ),
        in_specs=[vmem, vmem],
        out_specs=(hbm, hbm),
        scratch_shapes=[pltpu.SemaphoreType.DMA((9,))],
        compiler_params=pltpu.CompilerParams(vmem_limit_bytes=4 << 20),
    )(got, grad)


def solution(mesh):
    pixels = P(("gx", "gy"))
    placed = (
        P(None, None, "gx", "gy"), P(None, None, "gx", "gy"), P(None, "gx", "gy"),
        P(None, "gx", "gy"), P(), P(), pixels, P(("gx", "gy"), None), pixels, pixels, pixels,
    )
    return jax.shard_map(
        per_device,
        mesh=mesh,
        in_specs=placed,
        out_specs=(P(None, None, "gx", "gy"), P(None, ("gx", "gy"))),
        check_vma=False,
    )
```

```python
import jax
import jax.numpy as jnp
from jax import lax
from jax.experimental import pallas as pl
from jax.experimental.pallas import tpu as pltpu
from jax.sharding import PartitionSpec as P

MESH = pl.DeviceIdType.MESH
F32 = jnp.float32
BF16 = jnp.bfloat16
SEC, LEV, CX, CY = 40, 16, 8, 128
PIX = 2048
TILE = 1024
LCH = 4
BANDS = tuple((8 * b, 8) for b in range(5))
ORDERS = ((0, 1, 2), (1, 2, 0), (2, 0, 1), (0, 1, 2), (1, 2, 0))
GROUP_IN = 2
GROUP_OUT = 4
PLAN = (
    (0, 1), (1, 1), (2, 1), (3, 1), (4, 1), (0, 2), (1, 2), (2, 2), (3, 2), (4, 2),
)


def split(v):
    hi = v.astype(BF16).astype(F32)
    return hi, v - hi


def place():
    gx = lax.axis_index("gx")
    gy = lax.axis_index("gy")
    return lax.rem(gx, 4), gx // 4, gy // 2, lax.rem(gy, 2)


EAST, WEST, NORTH, SOUTH, KEEP = range(5)


def kernel(
    adj_h, conc_h, cx_h, cy_h, dif_ref, ker_h, col_h, own_h, slot_h, lev_h, wgt_h,
    out_ref, grad_ref,
    adj, conc, cx, cy, ker, col, own, slot, lev, wgt,
    coef, k3, k3t, rates, px, py, rx, ry, cells, hot, prof, pairs, held, contrib, contrib2, own2, slot2, pairs2, hot2,
    ds, r1, r2, lsem, ssem, rsem, fsem, gsem,
):
    gx = lax.axis_index("gx")
    gy = lax.axis_index("gy")
    x, y, z, c = place()
    mine = (x, y, z)
    half_peers = (
        (lax.rem(gx + 15, 16), gy),
        (lax.rem(gx + 1, 16), gy),
        (gx, lax.rem(gy + 7, 8)),
        (gx, lax.rem(gy + 1, 8)),
    )

    def at(axis, by):
        return lax.rem(mine[axis] + by + 4, 4)

    def dev(axis, by):
        xx = at(0, by) if axis == 0 else x
        yy = at(1, by) if axis == 1 else y
        zz = at(2, by) if axis == 2 else z
        return (yy * 4 + xx, zz * 2 + c)

    def spot(by):
        return (at(1, by[1]) * 4 + at(0, by[0]), at(2, by[2]) * 2 + c)

    sibling = (gx, z * 2 + 1 - c)
    loads = {}
    for i, (name, src, dst) in enumerate((
        ("cx", cx_h, cx), ("cy", cy_h, cy), ("adj", adj_h, adj), ("conc", conc_h, conc),
        ("ker", ker_h, ker), ("col", col_h, col), ("own", own_h, own), ("slot", slot_h, slot),
        ("lev", lev_h, lev), ("wgt", wgt_h, wgt),
    )):
        loads[name] = pltpu.make_async_copy(src, dst, lsem.at[i])
        loads[name].start()
    barrier = pltpu.get_barrier_semaphore()
    for peer in half_peers:
        pl.semaphore_signal(barrier, 1, device_id=peer, device_id_type=MESH)
    pl.semaphore_signal(barrier, 1, device_id=sibling, device_id_type=MESH)
    for dx in range(4):
        for dy in range(4):
            for dz in range(4):
                if 0 < (dx > 0) + (dy > 0) + (dz > 0) < 3:
                    pl.semaphore_signal(
                        barrier, 1, device_id=spot((dx, dy, dz)), device_id_type=MESH
                    )
    count = [0]
    done = []

    def send(src, dst, peer):
        n = count[0]
        count[0] += 1
        copy = pltpu.make_async_remote_copy(
            src, dst, ssem.at[n], rsem.at[n], device_id=peer, device_id_type=MESH
        )
        copy.start()
        done.append(copy)
        return copy

    loads["cx"].wait()
    loads["cy"].wait()

    def factors(l, carry):
        kap = dif_ref[l]
        a, b = cx[l], cy[l]
        coef[EAST, l] = jnp.maximum(a, 0.0) + kap
        coef[WEST, l] = jnp.maximum(-a, 0.0) + kap
        coef[NORTH, l] = jnp.maximum(b, 0.0) + kap
        coef[SOUTH, l] = jnp.maximum(-b, 0.0) + kap
        coef[KEEP, l] = 1.0 - jnp.abs(a) - jnp.abs(b) - 4.0 * kap
        return carry

    lax.fori_loop(0, LEV, factors, 0)
    loads["adj"].wait()
    first = coef[EAST, :, 0, :]
    last = coef[WEST, :, CX - 1, :]

    def fill(part):
        rows = slice(8 * part, 8 * part + 8)

        def one(k, carry):
            px[0, part, k] = adj[k, rows, 0, :] * first[rows]
            px[1, part, k] = adj[k, rows, CX - 1, :] * last[rows]
            return carry

        lax.fori_loop(0, SEC, one, 0, unroll=4)

    fill(0)
    fill(1)
    lane = lax.broadcasted_iota(jnp.int32, (SEC, CY), 1)
    row = lax.broadcasted_iota(jnp.int32, (SEC, CY), 0)

    def edge(l, carry):
        low, high = carry
        for i in range(CX):
            a = adj[:, l, i, :]
            q = l * CX + i
            s = pltpu.roll(a * coef[NORTH, l, pl.ds(i, 1), :], q, 1)
            n = pltpu.roll(a * coef[SOUTH, l, pl.ds(i, 1), :], q + 1, 1)
            low = jnp.where(lane == q, s, low)
            high = jnp.where(lane == q, n, high)
        return low, high

    zero = jnp.zeros((SEC, CY), F32)
    low, high = lax.fori_loop(0, LEV, edge, (zero, zero))
    py[0] = low
    py[1] = high

    pl.semaphore_wait(barrier, 41)
    sent_y = [send(py.at[i], ry.at[i], half_peers[2 + i]) for i in range(2)]
    sent_x = [
        [send(px.at[i, n], rx.at[i, n], half_peers[i]) for i in range(2)] for n in range(2)
    ]
    loads["own"].wait()
    loads["slot"].wait()
    sent_i = [send(own, own2, sibling), send(slot, slot2, sibling)]

    loads["ker"].wait()
    loads["conc"].wait()
    kh, kl = split(ker[...])
    k3[...] = jnp.concatenate([kh, kh, kl], axis=1).astype(BF16)
    kh, kl = split(ker[...].T)
    k3t[...] = jnp.concatenate([kh, kh, kl], axis=1).astype(BF16)
    def product(k, v):
        vh, vl = split(v)
        v3 = jnp.concatenate([vh, vl, vh], axis=0).astype(BF16)
        return jnp.dot(k[...], v3, preferred_element_type=F32)

    def rate(it, carry):
        cc = jnp.concatenate(
            [conc[:, it * 2 + g, i, :] for g in range(2) for i in range(CX)], axis=1
        )
        got = product(k3, cc)
        for g in range(2):
            base = pl.multiple_of((it * 2 + g) * SEC, SEC)
            rates[pl.ds(base, SEC), :] = got[:, g * CX * CY:(g + 1) * CX * CY]
        return carry

    lax.fori_loop(0, LEV // 2, rate, 0)
    for name in ("col", "lev", "wgt"):
        loads[name].wait()
    height = lax.broadcasted_iota(jnp.int32, (LEV, PIX), 0).astype(F32) - lev[...].astype(F32)
    shape = jnp.exp(-height * height / 8.0)
    prof[...] = shape / jnp.sum(shape, axis=0, keepdims=True) * wgt[...]
    def targets(owner, place_in, pair_out, hot_out):
        cell = owner[...] // 2
        pair_out[...] = jnp.broadcast_to((cell // 2).astype(F32), (16, PIX)).astype(BF16)
        want = (cell - cell // 2 * 2) * CY + place_in[...]
        want = jnp.where(owner[...] - cell * 2 == c, want, -1)
        for i in range(4):
            ids = lax.broadcasted_iota(jnp.int32, (64, PIX), 0) + i * 64
            hot_out[pl.ds(i * 64, 64), :] = jnp.where(ids == want, 1.0, 0.0).astype(BF16)

    targets(own, slot, pairs, hot)
    turned = lax.rem(col[...] + (CX - 1) * CY, CX * CY)

    def mark(i, carry):
        base = pl.multiple_of(i * 64, 64)
        ids = lax.broadcasted_iota(jnp.int32, (64, PIX), 0) + base
        cells[pl.ds(base, 64), :] = jnp.where(ids == turned, 1.0, 0.0).astype(BF16)
        return carry

    lax.fori_loop(0, CX * CY // 64, mark, 0)

    far_e = jnp.where(gx == 15, 0.0, 1.0)
    far_w = jnp.where(gx == 0, 0.0, 1.0)
    far_n = jnp.where(gy == 7, 0.0, 1.0)
    far_s = jnp.where(gy == 0, 0.0, 1.0)

    def levels(xs, group, start, stop):
        def step(it, carry):
            moved, ups, concs, turns = [], [], [], []
            for g in range(group):
                l = it * group + g
                turn = lax.rem(CY - l * CX, CY)
                hn = pltpu.roll(ry[0], turn, 1) * far_n
                hs = pltpu.roll(ry[1], turn, 1) * far_s

                def cf(kind, i):
                    return coef[kind, l, pl.ds(i, 1), :]

                for i in xs:
                    a = adj[:, l, i, :]
                    m = cf(KEEP, i) * a
                    if i < CX - 1:
                        m = m + cf(EAST, i + 1) * adj[:, l, i + 1, :]
                    else:
                        m = m + rx[0, l // 8, :, lax.rem(l, 8), :] * far_e
                    if i > 0:
                        m = m + cf(WEST, i - 1) * adj[:, l, i - 1, :]
                    else:
                        m = m + rx[1, l // 8, :, lax.rem(l, 8), :] * far_w
                    nh = pltpu.roll(hn, (CY - i) % CY, 1)
                    sh = pltpu.roll(hs, (CY - 1 - i) % CY, 1)
                    m = m + pltpu.roll(jnp.where(lane == 0, nh, cf(NORTH, i) * a), CY - 1, 1)
                    m = m + pltpu.roll(jnp.where(lane == CY - 1, sh, cf(SOUTH, i) * a), 1, 1)
                    nxt = jnp.where(row == SEC - 1, 0.0, pltpu.roll(m, SEC - 1, 0))
                    moved.append(m)
                    ups.append(nxt - m)
                    concs.append(conc[:, l, i, :])
                    base = pl.multiple_of(l * SEC, SEC)
                    turns.append(rates[pl.ds(base, SEC), i * CY:(i + 1) * CY])
            m = jnp.concatenate(moved, axis=1)
            up = jnp.concatenate(ups, axis=1)
            cc = jnp.concatenate(concs, axis=1)
            new = m + up * jnp.concatenate(turns, axis=1) + product(k3t, up * cc)
            rh, rl = split(new)
            both = jnp.concatenate([rh, rl], axis=0).astype(BF16)
            n = 0
            for g in range(group):
                l = it * group + g
                at_row = pl.ds(pl.multiple_of(l * 2 * SEC, 2 * SEC), 2 * SEC)
                for i in xs:
                    lanes = slice(n * CY, (n + 1) * CY)
                    spot = (i + CX - 1) % CX * CY
                    out_ref[:, l, i, :] = new[:, lanes]
                    held[at_row, spot:spot + CY] = both[:, lanes]
                    n += 1
            return carry

        lax.fori_loop(start, stop, step, 0)

    def gather(low, high, more):
        def tile(t, carry):
            where = pl.ds(pl.multiple_of(t * TILE, TILE), TILE)
            total = contrib[:, where] if more else jnp.zeros((SEC, TILE), F32)
            onehot = cells[low:high, where]
            for j in range(0, LEV, LCH):
                block = held[j * 2 * SEC:(j + LCH) * 2 * SEC, low:high]
                got = jnp.dot(block, onehot, preferred_element_type=F32)
                for l in range(LCH):
                    base = l * 2 * SEC
                    both = got[base:base + SEC] + got[base + SEC:base + 2 * SEC]
                    total = total + both * prof[pl.ds(j + l, 1), where]
            contrib[:, where] = total
            return carry

        lax.fori_loop(0, PIX // TILE, tile, 0)

    for copy in sent_y:
        copy.wait_recv()
    levels(range(1, CX - 1), GROUP_IN, 0, LEV // GROUP_IN)
    gather(0, 6 * CY, False)
    for copy in sent_i:
        copy.wait_recv()
    targets(own2, slot2, pairs2, hot2)
    for n in range(2):
        for copy in sent_x[n]:
            copy.wait_recv()
        levels((CX - 1, 0), GROUP_OUT, n * 8 // GROUP_OUT, (n + 1) * 8 // GROUP_OUT)
    gather(6 * CY, 8 * CY, True)
    swap = send(contrib, contrib2, sibling)

    dims = (((1,), (1,)), ((), ()))

    def scatter(b, values, pair_in, hot_in, more):
        low, size = BANDS[b]
        ch, cl = split(values[pl.ds(low, size), :])
        both = jnp.concatenate([ch, cl], axis=0).astype(BF16)
        none = jnp.zeros((16, PIX), BF16)
        for j in range(2):
            rows = jnp.concatenate(
                [jnp.where(pair_in[...] == float(j * 16 + i), both, none) for i in range(16)],
                axis=0,
            )
            got = lax.dot_general(rows, hot_in[...], dims, preferred_element_type=F32)
            for i in range(16):
                yy, xx, zz = j * 2 + i // 8, i // 2 % 4, i % 2 * 2
                one = got[i * 16:i * 16 + 8] + got[i * 16 + 8:i * 16 + 16]
                for k in range(2):
                    new = one[:, k * CY:(k + 1) * CY]
                    if more:
                        new = new + ds[b, yy, xx, zz + k]
                    ds[b, yy, xx, zz + k] = new

    def part(b, fixed):
        idx = [slice(None)] * 3
        for axis, value in fixed.items():
            idx[(1, 0, 2)[axis]] = value
        return ds.at[(b,) + tuple(idx)]

    sides = ((0, 1), (1, -1), (2, 2))

    def stage_c(b):
        scatter(b, contrib2, pairs2, hot2, True)
        a1 = ORDERS[b][0]
        return [send(part(b, {a1: at(a1, by)}), r1.at[b, i], dev(a1, by)) for i, by in sides]

    def stage_1(b, copies):
        a1, a2, a3 = ORDERS[b]
        for copy in copies:
            copy.wait_recv()
        here = part(b, {a1: mine[a1]})
        here[...] = here[...] + r1[b, 0] + r1[b, 1] + r1[b, 2]

        def one(i, carry):
            by = [0, 0, 0]
            by[a2] = i // 4
            by[a3] = lax.rem(i, 4)
            pltpu.make_async_remote_copy(
                ds.at[b, at(1, by[1]), at(0, by[0]), at(2, by[2])], r2.at[b, i],
                fsem.at[b], gsem.at[b], device_id=spot(by), device_id_type=MESH,
            ).start()
            return carry

        lax.fori_loop(1, 16, one, 0)

    def stage_2(b):
        start, size = BANDS[b]
        rest = r2.at[b, pl.ds(1, 15)]
        pltpu.make_async_copy(rest, rest, gsem.at[b]).wait()
        total = ds[b, y, x, z]
        for i in range(1, 16):
            total = total + r2[b, i]
        grad_ref[pl.ds(start, size), :] = total

    for b in range(5):
        scatter(b, contrib, pairs, hot, False)
    swap.wait_recv()
    work = [stage_c(b) for b in range(5)]
    for b, n in PLAN:
        if n == 1:
            stage_1(b, work[b])
        else:
            stage_2(b)
    for copy in done:
        copy.wait_send()
    for b in range(5):
        rest = r2.at[b, pl.ds(1, 15)]
        pltpu.make_async_copy(rest, rest, fsem.at[b]).wait()


def store_kernel(src, grad, dst, grad_dst, sems):
    copies = [
        pltpu.make_async_copy(src.at[pl.ds(5 * n, 5)], dst.at[pl.ds(5 * n, 5)], sems.at[n])
        for n in range(8)
    ]
    copies.append(pltpu.make_async_copy(grad, grad_dst, sems.at[8]))
    for copy in copies:
        copy.start()
    for copy in copies:
        copy.wait()


def per_device(
    adjoint, concentration, courant_x, courant_y, diffusion, coag_kernel,
    pixel_column, pixel_owner, pixel_slot, pixel_level, pixel_weight,
):
    vmem = pl.BlockSpec(memory_space=pltpu.VMEM)
    smem = pl.BlockSpec(memory_space=pltpu.SMEM)
    hbm = pl.BlockSpec(memory_space=pltpu.HBM)
    field = (SEC, LEV, CX, CY)
    plane = (LEV, CX, CY)

    ints = pltpu.VMEM((1, PIX), jnp.int32)
    got, grad = pl.pallas_call(
        kernel,
        out_shape=(
            jax.ShapeDtypeStruct(field, F32),
            jax.ShapeDtypeStruct((SEC, CY), F32),
        ),
        in_specs=[hbm, hbm, hbm, hbm, smem] + [hbm] * 6,
        out_specs=(vmem, vmem),
        scratch_shapes=[
            pltpu.VMEM(field, F32), pltpu.VMEM(field, F32),
            pltpu.VMEM(plane, F32), pltpu.VMEM(plane, F32),
            pltpu.VMEM((SEC, SEC), F32),
            ints, ints, ints, ints, pltpu.VMEM((1, PIX), F32),
            pltpu.VMEM((5,) + plane, F32),
            pltpu.VMEM((SEC, 3 * SEC), BF16), pltpu.VMEM((SEC, 3 * SEC), BF16),
            pltpu.VMEM((LEV * SEC, CX * CY), F32),
            pltpu.VMEM((2, 2, SEC, 8, CY), F32), pltpu.VMEM((2, SEC, CY), F32),
            pltpu.VMEM((2, 2, SEC, 8, CY), F32), pltpu.VMEM((2, SEC, CY), F32),
            pltpu.VMEM((CX * CY, PIX), BF16), pltpu.VMEM((2 * CY, PIX), BF16),
            pltpu.VMEM((LEV, PIX), F32), pltpu.VMEM((16, PIX), BF16),
            pltpu.VMEM((LEV * 2 * SEC, CX * CY), BF16),
            pltpu.VMEM((SEC, PIX), F32), pltpu.VMEM((SEC, PIX), F32),
            ints, ints, pltpu.VMEM((16, PIX), BF16), pltpu.VMEM((2 * CY, PIX), BF16),
            pltpu.VMEM((5, 4, 4, 4, 8, CY), F32),
            pltpu.VMEM((5, 3, 4, 4, 8, CY), F32),
            pltpu.VMEM((5, 16, 8, CY), F32),
            pltpu.SemaphoreType.DMA((10,)),
            pltpu.SemaphoreType.DMA((24,)),
            pltpu.SemaphoreType.DMA((24,)),
            pltpu.SemaphoreType.DMA((5,)),
            pltpu.SemaphoreType.DMA((5,)),
        ],
        compiler_params=pltpu.CompilerParams(
            collective_id=0, has_side_effects=True, vmem_limit_bytes=48 << 20
        ),
    )(*(pltpu.with_memory_space_constraint(v, pltpu.HBM) for v in (
        adjoint, concentration, courant_x, courant_y, diffusion, coag_kernel,
        pixel_column[None, :], pixel_owner[:, 0][None, :], pixel_slot[None, :],
        pixel_level[None, :], pixel_weight[None, :],
    )))
    return pl.pallas_call(
        store_kernel,
        out_shape=(
            jax.ShapeDtypeStruct(field, F32),
            jax.ShapeDtypeStruct((SEC, CY), F32),
        ),
        in_specs=[vmem, vmem],
        out_specs=(hbm, hbm),
        scratch_shapes=[pltpu.SemaphoreType.DMA((9,))],
        compiler_params=pltpu.CompilerParams(vmem_limit_bytes=4 << 20),
    )(got, grad)


def solution(mesh):
    pixels = P(("gx", "gy"))
    placed = (
        P(None, None, "gx", "gy"), P(None, None, "gx", "gy"), P(None, "gx", "gy"),
        P(None, "gx", "gy"), P(), P(), pixels, P(("gx", "gy"), None), pixels, pixels, pixels,
    )
    return jax.shard_map(
        per_device,
        mesh=mesh,
        in_specs=placed,
        out_specs=(P(None, None, "gx", "gy"), P(None, ("gx", "gy"))),
        check_vma=False,
    )
```

```python
import jax
import jax.numpy as jnp
from jax import lax
from jax.experimental import pallas as pl
from jax.experimental.pallas import tpu as pltpu
from jax.sharding import PartitionSpec as P

MESH = pl.DeviceIdType.MESH
F32 = jnp.float32
BF16 = jnp.bfloat16
SEC, LEV, CX, CY = 40, 16, 8, 128
PIX = 2048
TILE = 1024
LCH = 4
BANDS = tuple((8 * b, 8) for b in range(5))
ORDERS = ((0, 1, 2), (1, 2, 0), (2, 0, 1), (0, 1, 2), (1, 2, 0))
GROUP_IN = 2
GROUP_OUT = 4
PLAN = (
    (0, 1), (1, 1), (2, 1), (3, 1), (4, 1), (0, 2), (1, 2), (2, 2), (3, 2), (4, 2),
)


def split(v):
    hi = v.astype(BF16).astype(F32)
    return hi, v - hi


def place():
    gx = lax.axis_index("gx")
    gy = lax.axis_index("gy")
    return lax.rem(gx, 4), gx // 4, gy // 2, lax.rem(gy, 2)


EAST, WEST, NORTH, SOUTH, KEEP = range(5)


def kernel(
    adj_h, conc_h, cx_h, cy_h, dif_ref, ker_h, col_h, own_h, slot_h, lev_h, wgt_h,
    out_ref, grad_ref,
    adj, conc, cx, cy, ker, col, own, slot, lev, wgt,
    coef, k3, k3t, px, py, rx, ry, cells, hot, prof, pairs, held, contrib, contrib2, own2, slot2, pairs2, hot2,
    ds, r1, r2, lsem, ssem, rsem, fsem, gsem,
):
    gx = lax.axis_index("gx")
    gy = lax.axis_index("gy")
    x, y, z, c = place()
    mine = (x, y, z)
    half_peers = (
        (lax.rem(gx + 15, 16), gy),
        (lax.rem(gx + 1, 16), gy),
        (gx, lax.rem(gy + 7, 8)),
        (gx, lax.rem(gy + 1, 8)),
    )

    def at(axis, by):
        return lax.rem(mine[axis] + by + 4, 4)

    def dev(axis, by):
        xx = at(0, by) if axis == 0 else x
        yy = at(1, by) if axis == 1 else y
        zz = at(2, by) if axis == 2 else z
        return (yy * 4 + xx, zz * 2 + c)

    def spot(by):
        return (at(1, by[1]) * 4 + at(0, by[0]), at(2, by[2]) * 2 + c)

    sibling = (gx, z * 2 + 1 - c)
    loads = {}
    for i, (name, src, dst) in enumerate((
        ("cx", cx_h, cx), ("cy", cy_h, cy), ("adj", adj_h, adj), ("conc", conc_h, conc),
        ("ker", ker_h, ker), ("col", col_h, col), ("own", own_h, own), ("slot", slot_h, slot),
        ("lev", lev_h, lev), ("wgt", wgt_h, wgt),
    )):
        loads[name] = pltpu.make_async_copy(src, dst, lsem.at[i])
        loads[name].start()
    barrier = pltpu.get_barrier_semaphore()
    for peer in half_peers:
        pl.semaphore_signal(barrier, 1, device_id=peer, device_id_type=MESH)
    pl.semaphore_signal(barrier, 1, device_id=sibling, device_id_type=MESH)
    for dx in range(4):
        for dy in range(4):
            for dz in range(4):
                if 0 < (dx > 0) + (dy > 0) + (dz > 0) < 3:
                    pl.semaphore_signal(
                        barrier, 1, device_id=spot((dx, dy, dz)), device_id_type=MESH
                    )
    count = [0]
    done = []

    def send(src, dst, peer):
        n = count[0]
        count[0] += 1
        copy = pltpu.make_async_remote_copy(
            src, dst, ssem.at[n], rsem.at[n], device_id=peer, device_id_type=MESH
        )
        copy.start()
        done.append(copy)
        return copy

    loads["cx"].wait()
    loads["cy"].wait()

    def factors(l, carry):
        kap = dif_ref[l]
        a, b = cx[l], cy[l]
        coef[EAST, l] = jnp.maximum(a, 0.0) + kap
        coef[WEST, l] = jnp.maximum(-a, 0.0) + kap
        coef[NORTH, l] = jnp.maximum(b, 0.0) + kap
        coef[SOUTH, l] = jnp.maximum(-b, 0.0) + kap
        coef[KEEP, l] = 1.0 - jnp.abs(a) - jnp.abs(b) - 4.0 * kap
        return carry

    lax.fori_loop(0, LEV, factors, 0)
    loads["adj"].wait()
    first = coef[EAST, :, 0, :]
    last = coef[WEST, :, CX - 1, :]

    def fill(part):
        rows = slice(8 * part, 8 * part + 8)

        def one(k, carry):
            px[0, part, k] = adj[k, rows, 0, :] * first[rows]
            px[1, part, k] = adj[k, rows, CX - 1, :] * last[rows]
            return carry

        lax.fori_loop(0, SEC, one, 0, unroll=4)

    fill(0)
    fill(1)
    lane = lax.broadcasted_iota(jnp.int32, (SEC, CY), 1)
    row = lax.broadcasted_iota(jnp.int32, (SEC, CY), 0)

    def edge(l, carry):
        low, high = carry
        for i in range(CX):
            a = adj[:, l, i, :]
            q = l * CX + i
            s = pltpu.roll(a * coef[NORTH, l, pl.ds(i, 1), :], q, 1)
            n = pltpu.roll(a * coef[SOUTH, l, pl.ds(i, 1), :], q + 1, 1)
            low = jnp.where(lane == q, s, low)
            high = jnp.where(lane == q, n, high)
        return low, high

    zero = jnp.zeros((SEC, CY), F32)
    low, high = lax.fori_loop(0, LEV, edge, (zero, zero))
    py[0] = low
    py[1] = high

    pl.semaphore_wait(barrier, 41)
    sent_y = [send(py.at[i], ry.at[i], half_peers[2 + i]) for i in range(2)]
    sent_x = [
        [send(px.at[i, n], rx.at[i, n], half_peers[i]) for i in range(2)] for n in range(2)
    ]
    loads["own"].wait()
    loads["slot"].wait()
    sent_i = [send(own, own2, sibling), send(slot, slot2, sibling)]

    loads["ker"].wait()
    loads["conc"].wait()
    kh, kl = split(ker[...])
    k3[...] = jnp.concatenate([kh, kh, kl], axis=1).astype(BF16)
    kh, kl = split(ker[...].T)
    k3t[...] = jnp.concatenate([kh, kh, kl], axis=1).astype(BF16)
    def product(k, v):
        vh, vl = split(v)
        v3 = jnp.concatenate([vh, vl, vh], axis=0).astype(BF16)
        return jnp.dot(k[...], v3, preferred_element_type=F32)

    for name in ("col", "lev", "wgt"):
        loads[name].wait()
    height = lax.broadcasted_iota(jnp.int32, (LEV, PIX), 0).astype(F32) - lev[...].astype(F32)
    shape = jnp.exp(-height * height / 8.0)
    prof[...] = shape / jnp.sum(shape, axis=0, keepdims=True) * wgt[...]
    def targets(owner, place_in, pair_out, hot_out):
        cell = owner[...] // 2
        pair_out[...] = jnp.broadcast_to((cell // 2).astype(F32), (16, PIX)).astype(BF16)
        want = (cell - cell // 2 * 2) * CY + place_in[...]
        want = jnp.where(owner[...] - cell * 2 == c, want, -1)
        for i in range(4):
            ids = lax.broadcasted_iota(jnp.int32, (64, PIX), 0) + i * 64
            hot_out[pl.ds(i * 64, 64), :] = jnp.where(ids == want, 1.0, 0.0).astype(BF16)

    targets(own, slot, pairs, hot)
    turned = lax.rem(col[...] + (CX - 1) * CY, CX * CY)

    def mark(i, carry):
        base = pl.multiple_of(i * 64, 64)
        ids = lax.broadcasted_iota(jnp.int32, (64, PIX), 0) + base
        cells[pl.ds(base, 64), :] = jnp.where(ids == turned, 1.0, 0.0).astype(BF16)
        return carry

    lax.fori_loop(0, CX * CY // 64, mark, 0)

    far_e = jnp.where(gx == 15, 0.0, 1.0)
    far_w = jnp.where(gx == 0, 0.0, 1.0)
    far_n = jnp.where(gy == 7, 0.0, 1.0)
    far_s = jnp.where(gy == 0, 0.0, 1.0)

    def levels(xs, group, start, stop):
        def step(it, carry):
            moved, ups, concs = [], [], []
            for g in range(group):
                l = it * group + g
                turn = lax.rem(CY - l * CX, CY)
                hn = pltpu.roll(ry[0], turn, 1) * far_n
                hs = pltpu.roll(ry[1], turn, 1) * far_s

                def cf(kind, i):
                    return coef[kind, l, pl.ds(i, 1), :]

                for i in xs:
                    a = adj[:, l, i, :]
                    m = cf(KEEP, i) * a
                    if i < CX - 1:
                        m = m + cf(EAST, i + 1) * adj[:, l, i + 1, :]
                    else:
                        m = m + rx[0, l // 8, :, lax.rem(l, 8), :] * far_e
                    if i > 0:
                        m = m + cf(WEST, i - 1) * adj[:, l, i - 1, :]
                    else:
                        m = m + rx[1, l // 8, :, lax.rem(l, 8), :] * far_w
                    nh = pltpu.roll(hn, (CY - i) % CY, 1)
                    sh = pltpu.roll(hs, (CY - 1 - i) % CY, 1)
                    m = m + pltpu.roll(jnp.where(lane == 0, nh, cf(NORTH, i) * a), CY - 1, 1)
                    m = m + pltpu.roll(jnp.where(lane == CY - 1, sh, cf(SOUTH, i) * a), 1, 1)
                    nxt = jnp.where(row == SEC - 1, 0.0, pltpu.roll(m, SEC - 1, 0))
                    moved.append(m)
                    ups.append(nxt - m)
                    concs.append(conc[:, l, i, :])
            m = jnp.concatenate(moved, axis=1)
            up = jnp.concatenate(ups, axis=1)
            cc = jnp.concatenate(concs, axis=1)
            new = m + up * product(k3, cc) + product(k3t, up * cc)
            rh, rl = split(new)
            both = jnp.concatenate([rh, rl], axis=0).astype(BF16)
            n = 0
            for g in range(group):
                l = it * group + g
                at_row = pl.ds(pl.multiple_of(l * 2 * SEC, 2 * SEC), 2 * SEC)
                for i in xs:
                    lanes = slice(n * CY, (n + 1) * CY)
                    spot = (i + CX - 1) % CX * CY
                    out_ref[:, l, i, :] = new[:, lanes]
                    held[at_row, spot:spot + CY] = both[:, lanes]
                    n += 1
            return carry

        lax.fori_loop(start, stop, step, 0)

    def gather(low, high, more):
        def tile(t, carry):
            where = pl.ds(pl.multiple_of(t * TILE, TILE), TILE)
            total = contrib[:, where] if more else jnp.zeros((SEC, TILE), F32)
            onehot = cells[low:high, where]
            for j in range(0, LEV, LCH):
                block = held[j * 2 * SEC:(j + LCH) * 2 * SEC, low:high]
                got = jnp.dot(block, onehot, preferred_element_type=F32)
                for l in range(LCH):
                    base = l * 2 * SEC
                    both = got[base:base + SEC] + got[base + SEC:base + 2 * SEC]
                    total = total + both * prof[pl.ds(j + l, 1), where]
            contrib[:, where] = total
            return carry

        lax.fori_loop(0, PIX // TILE, tile, 0)

    for copy in sent_y:
        copy.wait_recv()
    levels(range(1, CX - 1), GROUP_IN, 0, LEV // GROUP_IN)
    gather(0, 6 * CY, False)
    for copy in sent_i:
        copy.wait_recv()
    targets(own2, slot2, pairs2, hot2)
    for n in range(2):
        for copy in sent_x[n]:
            copy.wait_recv()
        levels((CX - 1, 0), GROUP_OUT, n * 8 // GROUP_OUT, (n + 1) * 8 // GROUP_OUT)
    gather(6 * CY, 8 * CY, True)
    swap = send(contrib, contrib2, sibling)

    dims = (((1,), (1,)), ((), ()))

    def scatter(b, values, pair_in, hot_in, more):
        low, size = BANDS[b]
        ch, cl = split(values[pl.ds(low, size), :])
        both = jnp.concatenate([ch, cl], axis=0).astype(BF16)
        none = jnp.zeros((16, PIX), BF16)
        for j in range(2):
            rows = jnp.concatenate(
                [jnp.where(pair_in[...] == float(j * 16 + i), both, none) for i in range(16)],
                axis=0,
            )
            got = lax.dot_general(rows, hot_in[...], dims, preferred_element_type=F32)
            for i in range(16):
                yy, xx, zz = j * 2 + i // 8, i // 2 % 4, i % 2 * 2
                one = got[i * 16:i * 16 + 8] + got[i * 16 + 8:i * 16 + 16]
                for k in range(2):
                    new = one[:, k * CY:(k + 1) * CY]
                    if more:
                        new = new + ds[b, yy, xx, zz + k]
                    ds[b, yy, xx, zz + k] = new

    def part(b, fixed):
        idx = [slice(None)] * 3
        for axis, value in fixed.items():
            idx[(1, 0, 2)[axis]] = value
        return ds.at[(b,) + tuple(idx)]

    sides = ((0, 1), (1, -1), (2, 2))

    def stage_c(b):
        scatter(b, contrib2, pairs2, hot2, True)
        a1 = ORDERS[b][0]
        return [send(part(b, {a1: at(a1, by)}), r1.at[b, i], dev(a1, by)) for i, by in sides]

    def stage_1(b, copies):
        a1, a2, a3 = ORDERS[b]
        for copy in copies:
            copy.wait_recv()
        here = part(b, {a1: mine[a1]})
        here[...] = here[...] + r1[b, 0] + r1[b, 1] + r1[b, 2]

        def one(i, carry):
            by = [0, 0, 0]
            by[a2] = i // 4
            by[a3] = lax.rem(i, 4)
            pltpu.make_async_remote_copy(
                ds.at[b, at(1, by[1]), at(0, by[0]), at(2, by[2])], r2.at[b, i],
                fsem.at[b], gsem.at[b], device_id=spot(by), device_id_type=MESH,
            ).start()
            return carry

        lax.fori_loop(1, 16, one, 0)

    def stage_2(b):
        start, size = BANDS[b]
        rest = r2.at[b, pl.ds(1, 15)]
        pltpu.make_async_copy(rest, rest, gsem.at[b]).wait()
        total = ds[b, y, x, z]
        for i in range(1, 16):
            total = total + r2[b, i]
        grad_ref[pl.ds(start, size), :] = total

    for b in range(5):
        scatter(b, contrib, pairs, hot, False)
    swap.wait_recv()
    work = [stage_c(b) for b in range(5)]
    for b, n in PLAN:
        if n == 1:
            stage_1(b, work[b])
        else:
            stage_2(b)
    for copy in done:
        copy.wait_send()
    for b in range(5):
        rest = r2.at[b, pl.ds(1, 15)]
        pltpu.make_async_copy(rest, rest, fsem.at[b]).wait()


def store_kernel(src, grad, dst, grad_dst, sems):
    copies = [
        pltpu.make_async_copy(src.at[pl.ds(5 * n, 5)], dst.at[pl.ds(5 * n, 5)], sems.at[n])
        for n in range(8)
    ]
    copies.append(pltpu.make_async_copy(grad, grad_dst, sems.at[8]))
    for copy in copies:
        copy.start()
    for copy in copies:
        copy.wait()


def per_device(
    adjoint, concentration, courant_x, courant_y, diffusion, coag_kernel,
    pixel_column, pixel_owner, pixel_slot, pixel_level, pixel_weight,
):
    vmem = pl.BlockSpec(memory_space=pltpu.VMEM)
    smem = pl.BlockSpec(memory_space=pltpu.SMEM)
    hbm = pl.BlockSpec(memory_space=pltpu.HBM)
    field = (SEC, LEV, CX, CY)
    plane = (LEV, CX, CY)

    ints = pltpu.VMEM((1, PIX), jnp.int32)
    got, grad = pl.pallas_call(
        kernel,
        out_shape=(
            jax.ShapeDtypeStruct(field, F32),
            jax.ShapeDtypeStruct((SEC, CY), F32),
        ),
        in_specs=[hbm, hbm, hbm, hbm, smem] + [hbm] * 6,
        out_specs=(vmem, vmem),
        scratch_shapes=[
            pltpu.VMEM(field, F32), pltpu.VMEM(field, F32),
            pltpu.VMEM(plane, F32), pltpu.VMEM(plane, F32),
            pltpu.VMEM((SEC, SEC), F32),
            ints, ints, ints, ints, pltpu.VMEM((1, PIX), F32),
            pltpu.VMEM((5,) + plane, F32),
            pltpu.VMEM((SEC, 3 * SEC), BF16), pltpu.VMEM((SEC, 3 * SEC), BF16),
            pltpu.VMEM((2, 2, SEC, 8, CY), F32), pltpu.VMEM((2, SEC, CY), F32),
            pltpu.VMEM((2, 2, SEC, 8, CY), F32), pltpu.VMEM((2, SEC, CY), F32),
            pltpu.VMEM((CX * CY, PIX), BF16), pltpu.VMEM((2 * CY, PIX), BF16),
            pltpu.VMEM((LEV, PIX), F32), pltpu.VMEM((16, PIX), BF16),
            pltpu.VMEM((LEV * 2 * SEC, CX * CY), BF16),
            pltpu.VMEM((SEC, PIX), F32), pltpu.VMEM((SEC, PIX), F32),
            ints, ints, pltpu.VMEM((16, PIX), BF16), pltpu.VMEM((2 * CY, PIX), BF16),
            pltpu.VMEM((5, 4, 4, 4, 8, CY), F32),
            pltpu.VMEM((5, 3, 4, 4, 8, CY), F32),
            pltpu.VMEM((5, 16, 8, CY), F32),
            pltpu.SemaphoreType.DMA((10,)),
            pltpu.SemaphoreType.DMA((24,)),
            pltpu.SemaphoreType.DMA((24,)),
            pltpu.SemaphoreType.DMA((5,)),
            pltpu.SemaphoreType.DMA((5,)),
        ],
        compiler_params=pltpu.CompilerParams(
            collective_id=0, has_side_effects=True, vmem_limit_bytes=48 << 20
        ),
    )(*(pltpu.with_memory_space_constraint(v, pltpu.HBM) for v in (
        adjoint, concentration, courant_x, courant_y, diffusion, coag_kernel,
        pixel_column[None, :], pixel_owner[:, 0][None, :], pixel_slot[None, :],
        pixel_level[None, :], pixel_weight[None, :],
    )))
    return pl.pallas_call(
        store_kernel,
        out_shape=(
            jax.ShapeDtypeStruct(field, F32),
            jax.ShapeDtypeStruct((SEC, CY), F32),
        ),
        in_specs=[vmem, vmem],
        out_specs=(hbm, hbm),
        scratch_shapes=[pltpu.SemaphoreType.DMA((9,))],
        compiler_params=pltpu.CompilerParams(vmem_limit_bytes=4 << 20),
    )(got, grad)


def solution(mesh):
    pixels = P(("gx", "gy"))
    placed = (
        P(None, None, "gx", "gy"), P(None, None, "gx", "gy"), P(None, "gx", "gy"),
        P(None, "gx", "gy"), P(), P(), pixels, P(("gx", "gy"), None), pixels, pixels, pixels,
    )
    return jax.shard_map(
        per_device,
        mesh=mesh,
        in_specs=placed,
        out_specs=(P(None, None, "gx", "gy"), P(None, ("gx", "gy"))),
        check_vma=False,
    )
```

```python
import jax
import jax.numpy as jnp
from jax import lax
from jax.experimental import pallas as pl
from jax.experimental.pallas import tpu as pltpu
from jax.sharding import PartitionSpec as P

MESH = pl.DeviceIdType.MESH
F32 = jnp.float32
BF16 = jnp.bfloat16
SEC, LEV, CX, CY = 40, 16, 8, 128
PIX = 2048
TILE = 1024
LCH = 4
BANDS = tuple((8 * b, 8) for b in range(5))
ORDERS = ((0, 1, 2), (1, 2, 0), (2, 0, 1), (0, 1, 2), (1, 2, 0))
GROUP_IN = 2
GROUP_OUT = 8
PLAN = (
    (0, 1), (1, 1), (2, 1), (3, 1), (4, 1), (0, 2), (1, 2), (2, 2), (3, 2), (4, 2),
)


def split(v):
    hi = v.astype(BF16).astype(F32)
    return hi, v - hi


def place():
    gx = lax.axis_index("gx")
    gy = lax.axis_index("gy")
    return lax.rem(gx, 4), gx // 4, gy // 2, lax.rem(gy, 2)


EAST, WEST, NORTH, SOUTH, KEEP = range(5)


def kernel(
    adj_h, conc_h, cx_h, cy_h, dif_ref, ker_h, col_h, own_h, slot_h, lev_h, wgt_h,
    out_ref, grad_ref,
    adj, conc, cx, cy, ker, col, own, slot, lev, wgt,
    coef, k3, k3t, px, py, rx, ry, cells, hot, prof, pairs, held, contrib, contrib2, own2, slot2, pairs2, hot2,
    ds, r1, r2, lsem, ssem, rsem, fsem, gsem,
):
    gx = lax.axis_index("gx")
    gy = lax.axis_index("gy")
    x, y, z, c = place()
    mine = (x, y, z)
    half_peers = (
        (lax.rem(gx + 15, 16), gy),
        (lax.rem(gx + 1, 16), gy),
        (gx, lax.rem(gy + 7, 8)),
        (gx, lax.rem(gy + 1, 8)),
    )

    def at(axis, by):
        return lax.rem(mine[axis] + by + 4, 4)

    def dev(axis, by):
        xx = at(0, by) if axis == 0 else x
        yy = at(1, by) if axis == 1 else y
        zz = at(2, by) if axis == 2 else z
        return (yy * 4 + xx, zz * 2 + c)

    def spot(by):
        return (at(1, by[1]) * 4 + at(0, by[0]), at(2, by[2]) * 2 + c)

    sibling = (gx, z * 2 + 1 - c)
    loads = {}
    for i, (name, src, dst) in enumerate((
        ("cx", cx_h, cx), ("cy", cy_h, cy), ("adj", adj_h, adj), ("conc", conc_h, conc),
        ("ker", ker_h, ker), ("col", col_h, col), ("own", own_h, own), ("slot", slot_h, slot),
        ("lev", lev_h, lev), ("wgt", wgt_h, wgt),
    )):
        loads[name] = pltpu.make_async_copy(src, dst, lsem.at[i])
        loads[name].start()
    barrier = pltpu.get_barrier_semaphore()
    for peer in half_peers:
        pl.semaphore_signal(barrier, 1, device_id=peer, device_id_type=MESH)
    pl.semaphore_signal(barrier, 1, device_id=sibling, device_id_type=MESH)
    for dx in range(4):
        for dy in range(4):
            for dz in range(4):
                if 0 < (dx > 0) + (dy > 0) + (dz > 0) < 3:
                    pl.semaphore_signal(
                        barrier, 1, device_id=spot((dx, dy, dz)), device_id_type=MESH
                    )
    count = [0]
    done = []

    def send(src, dst, peer):
        n = count[0]
        count[0] += 1
        copy = pltpu.make_async_remote_copy(
            src, dst, ssem.at[n], rsem.at[n], device_id=peer, device_id_type=MESH
        )
        copy.start()
        done.append(copy)
        return copy

    loads["cx"].wait()
    loads["cy"].wait()

    def factors(l, carry):
        kap = dif_ref[l]
        a, b = cx[l], cy[l]
        coef[EAST, l] = jnp.maximum(a, 0.0) + kap
        coef[WEST, l] = jnp.maximum(-a, 0.0) + kap
        coef[NORTH, l] = jnp.maximum(b, 0.0) + kap
        coef[SOUTH, l] = jnp.maximum(-b, 0.0) + kap
        coef[KEEP, l] = 1.0 - jnp.abs(a) - jnp.abs(b) - 4.0 * kap
        return carry

    lax.fori_loop(0, LEV, factors, 0)
    loads["adj"].wait()
    first = coef[EAST, :, 0, :]
    last = coef[WEST, :, CX - 1, :]

    def fill(part):
        rows = slice(8 * part, 8 * part + 8)

        def one(k, carry):
            px[0, part, k] = adj[k, rows, 0, :] * first[rows]
            px[1, part, k] = adj[k, rows, CX - 1, :] * last[rows]
            return carry

        lax.fori_loop(0, SEC, one, 0, unroll=4)

    fill(0)
    fill(1)
    lane = lax.broadcasted_iota(jnp.int32, (SEC, CY), 1)
    row = lax.broadcasted_iota(jnp.int32, (SEC, CY), 0)

    def edge(l, carry):
        low, high = carry
        for i in range(CX):
            a = adj[:, l, i, :]
            q = l * CX + i
            s = pltpu.roll(a * coef[NORTH, l, pl.ds(i, 1), :], q, 1)
            n = pltpu.roll(a * coef[SOUTH, l, pl.ds(i, 1), :], q + 1, 1)
            low = jnp.where(lane == q, s, low)
            high = jnp.where(lane == q, n, high)
        return low, high

    zero = jnp.zeros((SEC, CY), F32)
    low, high = lax.fori_loop(0, LEV, edge, (zero, zero))
    py[0] = low
    py[1] = high

    pl.semaphore_wait(barrier, 41)
    sent_y = [send(py.at[i], ry.at[i], half_peers[2 + i]) for i in range(2)]
    sent_x = [
        [send(px.at[i, n], rx.at[i, n], half_peers[i]) for i in range(2)] for n in range(2)
    ]
    loads["own"].wait()
    loads["slot"].wait()
    sent_i = [send(own, own2, sibling), send(slot, slot2, sibling)]

    loads["ker"].wait()
    loads["conc"].wait()
    kh, kl = split(ker[...])
    k3[...] = jnp.concatenate([kh, kh, kl], axis=1).astype(BF16)
    kh, kl = split(ker[...].T)
    k3t[...] = jnp.concatenate([kh, kh, kl], axis=1).astype(BF16)
    def product(k, v):
        vh, vl = split(v)
        v3 = jnp.concatenate([vh, vl, vh], axis=0).astype(BF16)
        return jnp.dot(k[...], v3, preferred_element_type=F32)

    for name in ("col", "lev", "wgt"):
        loads[name].wait()
    height = lax.broadcasted_iota(jnp.int32, (LEV, PIX), 0).astype(F32) - lev[...].astype(F32)
    shape = jnp.exp(-height * height / 8.0)
    prof[...] = shape / jnp.sum(shape, axis=0, keepdims=True) * wgt[...]
    def targets(owner, place_in, pair_out, hot_out):
        cell = owner[...] // 2
        pair_out[...] = jnp.broadcast_to((cell // 2).astype(F32), (16, PIX)).astype(BF16)
        want = (cell - cell // 2 * 2) * CY + place_in[...]
        want = jnp.where(owner[...] - cell * 2 == c, want, -1)
        for i in range(4):
            ids = lax.broadcasted_iota(jnp.int32, (64, PIX), 0) + i * 64
            hot_out[pl.ds(i * 64, 64), :] = jnp.where(ids == want, 1.0, 0.0).astype(BF16)

    targets(own, slot, pairs, hot)
    turned = lax.rem(col[...] + (CX - 1) * CY, CX * CY)

    def mark(i, carry):
        base = pl.multiple_of(i * 64, 64)
        ids = lax.broadcasted_iota(jnp.int32, (64, PIX), 0) + base
        cells[pl.ds(base, 64), :] = jnp.where(ids == turned, 1.0, 0.0).astype(BF16)
        return carry

    lax.fori_loop(0, CX * CY // 64, mark, 0)

    far_e = jnp.where(gx == 15, 0.0, 1.0)
    far_w = jnp.where(gx == 0, 0.0, 1.0)
    far_n = jnp.where(gy == 7, 0.0, 1.0)
    far_s = jnp.where(gy == 0, 0.0, 1.0)

    def levels(xs, group, start, stop):
        def step(it, carry):
            moved, ups, concs = [], [], []
            for g in range(group):
                l = it * group + g
                turn = lax.rem(CY - l * CX, CY)
                hn = pltpu.roll(ry[0], turn, 1) * far_n
                hs = pltpu.roll(ry[1], turn, 1) * far_s

                def cf(kind, i):
                    return coef[kind, l, pl.ds(i, 1), :]

                for i in xs:
                    a = adj[:, l, i, :]
                    m = cf(KEEP, i) * a
                    if i < CX - 1:
                        m = m + cf(EAST, i + 1) * adj[:, l, i + 1, :]
                    else:
                        m = m + rx[0, l // 8, :, lax.rem(l, 8), :] * far_e
                    if i > 0:
                        m = m + cf(WEST, i - 1) * adj[:, l, i - 1, :]
                    else:
                        m = m + rx[1, l // 8, :, lax.rem(l, 8), :] * far_w
                    nh = pltpu.roll(hn, (CY - i) % CY, 1)
                    sh = pltpu.roll(hs, (CY - 1 - i) % CY, 1)
                    m = m + pltpu.roll(jnp.where(lane == 0, nh, cf(NORTH, i) * a), CY - 1, 1)
                    m = m + pltpu.roll(jnp.where(lane == CY - 1, sh, cf(SOUTH, i) * a), 1, 1)
                    nxt = jnp.where(row == SEC - 1, 0.0, pltpu.roll(m, SEC - 1, 0))
                    moved.append(m)
                    ups.append(nxt - m)
                    concs.append(conc[:, l, i, :])
            m = jnp.concatenate(moved, axis=1)
            up = jnp.concatenate(ups, axis=1)
            cc = jnp.concatenate(concs, axis=1)
            new = m + up * product(k3, cc) + product(k3t, up * cc)
            rh, rl = split(new)
            both = jnp.concatenate([rh, rl], axis=0).astype(BF16)
            n = 0
            for g in range(group):
                l = it * group + g
                at_row = pl.ds(pl.multiple_of(l * 2 * SEC, 2 * SEC), 2 * SEC)
                for i in xs:
                    lanes = slice(n * CY, (n + 1) * CY)
                    spot = (i + CX - 1) % CX * CY
                    out_ref[:, l, i, :] = new[:, lanes]
                    held[at_row, spot:spot + CY] = both[:, lanes]
                    n += 1
            return carry

        lax.fori_loop(start, stop, step, 0)

    def gather(low, high, more):
        def tile(t, carry):
            where = pl.ds(pl.multiple_of(t * TILE, TILE), TILE)
            total = contrib[:, where] if more else jnp.zeros((SEC, TILE), F32)
            onehot = cells[low:high, where]
            for j in range(0, LEV, LCH):
                block = held[j * 2 * SEC:(j + LCH) * 2 * SEC, low:high]
                got = jnp.dot(block, onehot, preferred_element_type=F32)
                for l in range(LCH):
                    base = l * 2 * SEC
                    both = got[base:base + SEC] + got[base + SEC:base + 2 * SEC]
                    total = total + both * prof[pl.ds(j + l, 1), where]
            contrib[:, where] = total
            return carry

        lax.fori_loop(0, PIX // TILE, tile, 0)

    for copy in sent_y:
        copy.wait_recv()
    levels(range(1, CX - 1), GROUP_IN, 0, LEV // GROUP_IN)
    gather(0, 6 * CY, False)
    for copy in sent_i:
        copy.wait_recv()
    targets(own2, slot2, pairs2, hot2)
    for n in range(2):
        for copy in sent_x[n]:
            copy.wait_recv()
        levels((CX - 1, 0), GROUP_OUT, n * 8 // GROUP_OUT, (n + 1) * 8 // GROUP_OUT)
    gather(6 * CY, 8 * CY, True)
    swap = send(contrib, contrib2, sibling)

    dims = (((1,), (1,)), ((), ()))

    def scatter(b, values, pair_in, hot_in, more):
        low, size = BANDS[b]
        ch, cl = split(values[pl.ds(low, size), :])
        both = jnp.concatenate([ch, cl], axis=0).astype(BF16)
        none = jnp.zeros((16, PIX), BF16)
        for j in range(2):
            rows = jnp.concatenate(
                [jnp.where(pair_in[...] == float(j * 16 + i), both, none) for i in range(16)],
                axis=0,
            )
            got = lax.dot_general(rows, hot_in[...], dims, preferred_element_type=F32)
            for i in range(16):
                yy, xx, zz = j * 2 + i // 8, i // 2 % 4, i % 2 * 2
                one = got[i * 16:i * 16 + 8] + got[i * 16 + 8:i * 16 + 16]
                for k in range(2):
                    new = one[:, k * CY:(k + 1) * CY]
                    if more:
                        new = new + ds[b, yy, xx, zz + k]
                    ds[b, yy, xx, zz + k] = new

    def part(b, fixed):
        idx = [slice(None)] * 3
        for axis, value in fixed.items():
            idx[(1, 0, 2)[axis]] = value
        return ds.at[(b,) + tuple(idx)]

    sides = ((2, 2), (0, 1), (1, -1))

    def stage_c(b):
        scatter(b, contrib2, pairs2, hot2, True)
        a1 = ORDERS[b][0]
        return [send(part(b, {a1: at(a1, by)}), r1.at[b, i], dev(a1, by)) for i, by in sides]

    def stage_1(b, copies):
        a1, a2, a3 = ORDERS[b]
        for copy in copies:
            copy.wait_recv()
        here = part(b, {a1: mine[a1]})
        here[...] = here[...] + r1[b, 0] + r1[b, 1] + r1[b, 2]

        def one(i, carry):
            by = [0, 0, 0]
            by[a2] = i // 4
            by[a3] = lax.rem(i, 4)
            pltpu.make_async_remote_copy(
                ds.at[b, at(1, by[1]), at(0, by[0]), at(2, by[2])], r2.at[b, i],
                fsem.at[b], gsem.at[b], device_id=spot(by), device_id_type=MESH,
            ).start()
            return carry

        lax.fori_loop(1, 16, one, 0)

    def stage_2(b):
        start, size = BANDS[b]
        rest = r2.at[b, pl.ds(1, 15)]
        pltpu.make_async_copy(rest, rest, gsem.at[b]).wait()
        total = ds[b, y, x, z]
        for i in range(1, 16):
            total = total + r2[b, i]
        grad_ref[pl.ds(start, size), :] = total

    for b in range(5):
        scatter(b, contrib, pairs, hot, False)
    swap.wait_recv()
    work = [stage_c(b) for b in range(5)]
    for b, n in PLAN:
        if n == 1:
            stage_1(b, work[b])
        else:
            stage_2(b)
    for copy in done:
        copy.wait_send()
    for b in range(5):
        rest = r2.at[b, pl.ds(1, 15)]
        pltpu.make_async_copy(rest, rest, fsem.at[b]).wait()


def store_kernel(src, grad, dst, grad_dst, sems):
    copies = [
        pltpu.make_async_copy(src.at[pl.ds(5 * n, 5)], dst.at[pl.ds(5 * n, 5)], sems.at[n])
        for n in range(8)
    ]
    copies.append(pltpu.make_async_copy(grad, grad_dst, sems.at[8]))
    for copy in copies:
        copy.start()
    for copy in copies:
        copy.wait()


def per_device(
    adjoint, concentration, courant_x, courant_y, diffusion, coag_kernel,
    pixel_column, pixel_owner, pixel_slot, pixel_level, pixel_weight,
):
    vmem = pl.BlockSpec(memory_space=pltpu.VMEM)
    smem = pl.BlockSpec(memory_space=pltpu.SMEM)
    hbm = pl.BlockSpec(memory_space=pltpu.HBM)
    field = (SEC, LEV, CX, CY)
    plane = (LEV, CX, CY)

    ints = pltpu.VMEM((1, PIX), jnp.int32)
    got, grad = pl.pallas_call(
        kernel,
        out_shape=(
            jax.ShapeDtypeStruct(field, F32),
            jax.ShapeDtypeStruct((SEC, CY), F32),
        ),
        in_specs=[hbm, hbm, hbm, hbm, smem] + [hbm] * 6,
        out_specs=(vmem, vmem),
        scratch_shapes=[
            pltpu.VMEM(field, F32), pltpu.VMEM(field, F32),
            pltpu.VMEM(plane, F32), pltpu.VMEM(plane, F32),
            pltpu.VMEM((SEC, SEC), F32),
            ints, ints, ints, ints, pltpu.VMEM((1, PIX), F32),
            pltpu.VMEM((5,) + plane, F32),
            pltpu.VMEM((SEC, 3 * SEC), BF16), pltpu.VMEM((SEC, 3 * SEC), BF16),
            pltpu.VMEM((2, 2, SEC, 8, CY), F32), pltpu.VMEM((2, SEC, CY), F32),
            pltpu.VMEM((2, 2, SEC, 8, CY), F32), pltpu.VMEM((2, SEC, CY), F32),
            pltpu.VMEM((CX * CY, PIX), BF16), pltpu.VMEM((2 * CY, PIX), BF16),
            pltpu.VMEM((LEV, PIX), F32), pltpu.VMEM((16, PIX), BF16),
            pltpu.VMEM((LEV * 2 * SEC, CX * CY), BF16),
            pltpu.VMEM((SEC, PIX), F32), pltpu.VMEM((SEC, PIX), F32),
            ints, ints, pltpu.VMEM((16, PIX), BF16), pltpu.VMEM((2 * CY, PIX), BF16),
            pltpu.VMEM((5, 4, 4, 4, 8, CY), F32),
            pltpu.VMEM((5, 3, 4, 4, 8, CY), F32),
            pltpu.VMEM((5, 16, 8, CY), F32),
            pltpu.SemaphoreType.DMA((10,)),
            pltpu.SemaphoreType.DMA((24,)),
            pltpu.SemaphoreType.DMA((24,)),
            pltpu.SemaphoreType.DMA((5,)),
            pltpu.SemaphoreType.DMA((5,)),
        ],
        compiler_params=pltpu.CompilerParams(
            collective_id=0, has_side_effects=True, vmem_limit_bytes=48 << 20
        ),
    )(*(pltpu.with_memory_space_constraint(v, pltpu.HBM) for v in (
        adjoint, concentration, courant_x, courant_y, diffusion, coag_kernel,
        pixel_column[None, :], pixel_owner[:, 0][None, :], pixel_slot[None, :],
        pixel_level[None, :], pixel_weight[None, :],
    )))
    return pl.pallas_call(
        store_kernel,
        out_shape=(
            jax.ShapeDtypeStruct(field, F32),
            jax.ShapeDtypeStruct((SEC, CY), F32),
        ),
        in_specs=[vmem, vmem],
        out_specs=(hbm, hbm),
        scratch_shapes=[pltpu.SemaphoreType.DMA((9,))],
        compiler_params=pltpu.CompilerParams(vmem_limit_bytes=4 << 20),
    )(got, grad)


def solution(mesh):
    pixels = P(("gx", "gy"))
    placed = (
        P(None, None, "gx", "gy"), P(None, None, "gx", "gy"), P(None, "gx", "gy"),
        P(None, "gx", "gy"), P(), P(), pixels, P(("gx", "gy"), None), pixels, pixels, pixels,
    )
    return jax.shard_map(
        per_device,
        mesh=mesh,
        in_specs=placed,
        out_specs=(P(None, None, "gx", "gy"), P(None, ("gx", "gy"))),
        check_vma=False,
    )
```
